128 devices in a mesh: reg: 8 (over x, core), dam: 16 (over z, y).
Axes of the slice: x: 4, y: 4, z: 4, core: 2. Of those that a mesh axis runs over, the one named last changes fastest.
Arguments:
- history: bfloat16 [16384, 384], P(('reg', 'dam')), may hold values from -6 to 6
- routes: int32 [16384, 2], P(('reg', 'dam')), may hold values from 0 to 127, all different within a row; in each aligned block of 128 rows (0 to 127, 128 to 255, ...) at most 4 rows name the same one
- dam_field: bfloat16 [65536, 384], P(('reg', 'dam')), may hold values from -6 to 6
- conn_free: int32 [8192, 64], P(('reg', 'dam')), may hold values from 0 to 511
- conn_dam: int32 [8192, 64], P(('reg', 'dam')), may hold values from 0 to 511
- stiff_ref: bfloat16 [192, 192], replicated, may hold values from -0.4375 to 0.4375
- stiff_coef: float32 [8192], P(('reg', 'dam')), may hold values from 0.25 to 1
- mass_coef: float32 [8192], P(('reg', 'dam')), may hold values from 0.02 to 0.1
- reg_step: float32 [16384], P(('reg', 'dam')), may hold values from 0.05 to 0.2
- dam_step: float32 [65536], P(('reg', 'dam')), may hold values from 0.05 to 0.2
Outputs:
- history_out: bfloat16 [16384, 384], P(('reg', 'dam'))
- returned_force: float32 [16384, 384], P(('reg', 'dam'))
- dam_out: bfloat16 [65536, 384], P(('reg', 'dam'))
The draws below stay inside these ranges and needn't reach their ends.
Inputs may be any that keep to these rules, and one draw needn't show every extreme that they name: `routes`: in the rows of one device no device number appears more than 4 times; some number appears exactly 4 times in some devices' rows.
All inputs are finite; a program needn't handle non-finite values.
Results may differ from the reference program's by a relative error of at most 0.0047.
Values may be sent and summed in bfloat16 or wider, within the bound.
A program may use at most 64 MiB of HBM per device.

```python
import math
import jax
import jax.numpy as jnp
import numpy as np
from jax import lax

SAMPLES = 128
NODES = 64
ROUNDS = 2
RB_DEV = 128
ELEM_DEV = 64
DNODE_DEV = 512
CAP = 4
RB_TOTAL = 16384
ELEM_TOTAL = 8192
DNODE_TOTAL = 65536
DEVICES = 128


def with_ends(values, own_key, smallest, top_value):
    dims = values.shape
    index_at = [jax.random.randint(jax.random.fold_in(own_key, axis), (), 0, dims[axis]) for axis in range(len(dims))]
    values = values.at[tuple(index_at)].set(smallest)
    longest = dims.index(max(dims))
    index_at[longest] = (index_at[longest] + 1) % dims[longest]
    return values.at[tuple(index_at)].set(top_value)


def steps_of(own_key, extent, split, least, top_value):
    level, own = 1.0, jax.random.fold_in(own_key, 6)
    for axis_at, parts in split:
        steps = jnp.exp(jax.random.uniform(jax.random.fold_in(own, axis_at), (parts,), jnp.float32, least / len(split), top_value / len(split)))
        level = level * jnp.repeat(steps, extent[axis_at] // parts).reshape([-1 if axis == axis_at else 1 for axis in range(len(extent))])
    return level


def deal_out(rng, own, number, rows, number_of, top, reach, skew):
    ranking = jax.random.permutation(rng, number_of)
    packed, common = load_shares(number_of, rows * top, reach, skew, True), load_shares(number_of, rows * top, reach, skew, False)
    places = jnp.arange(number_of)

    def named(tallies, turn):
        used = int((tallies > 0).sum())
        fixed = max(1, used // 4)
        passed = fixed + (places - fixed + turn * (used - fixed)) % max(1, number_of - fixed)
        return jnp.zeros((number_of,), jnp.int32).at[ranking[jnp.where(places < fixed, places, passed)]].set(jnp.asarray(tallies, jnp.int32))

    tallies = jnp.where(number % 4 == 0, named(packed, number // 4), named(common, number - number // 4 - 1))
    mixed = jax.random.permutation(jax.random.fold_in(own, 3), number_of)
    donor, receiver = mixed[0:number_of // 2 * 2:2], mixed[1:number_of // 2 * 2:2]
    margin = jnp.minimum(tallies[donor] - 1, reach - tallies[receiver]) // 2
    margin = jnp.where((donor == ranking[0]) | (receiver == ranking[0]) | (tallies[receiver] == 0), 0, jnp.maximum(margin, 0))
    passed = jax.random.randint(jax.random.fold_in(own, 4), (number_of // 2,), 0, 1 << 20) % (margin + 1)
    tallies = tallies.at[donor].add(-passed).at[receiver].add(passed)
    members = jnp.searchsorted(jnp.cumsum(tallies), jnp.arange(rows * top), side="right").astype(jnp.int32)
    grid = members.reshape(top, rows).T
    grid = grid[jax.random.permutation(jax.random.fold_in(own, 1), rows)]
    turn = jax.random.randint(jax.random.fold_in(own, 2), (rows, 1), 0, top)
    return jnp.take_along_axis(grid, (jnp.arange(top)[None, :] + turn) % top, axis=1)


def load_shares(amount, total, bound, lean, full):
    weights = [(1 << 20) // math.isqrt(standing ** lean) + 1 for standing in range(1, amount + 1)]
    largest = bound if full else min(bound, max(-(-total // amount), total * weights[0] // sum(weights)))
    least = 1 if total - largest >= amount - 1 else 0
    given, rest = [largest] + [least] * (amount - 1), total - largest - least * (amount - 1)
    while rest > 0:
        movable = [i for i in range(1, amount) if given[i] < largest] or [i for i in range(1, amount) if given[i] < bound]
        mass, remaining = sum([weights[i] for i in movable]), rest
        for i in movable:
            extra = min(bound - given[i], max(1, remaining * weights[i] // mass), rest)
            given[i] = given[i] + extra
            rest = rest - extra
    return np.array(given)


def centred(stream_key, extent, spread, reach, cuts=(), held_as=jnp.bfloat16):
    level = steps_of(stream_key, extent, cuts, -0.22, 0.18) if cuts else 1.0
    values = jax.random.normal(stream_key, extent, jnp.float32) * spread * level
    return jnp.minimum(jnp.maximum(values, -reach), reach).astype(held_as)


def setup_inputs(seed: int = 0) -> dict:
    streams_of = jax.random.split(jax.random.key(seed), 11)
    history = centred(streams_of[0], (RB_TOTAL, 3 * SAMPLES), 1.0, 6.0, ((0, 128),))
    routes_keys = jax.random.split(jax.random.fold_in(streams_of[1], 1), RB_TOTAL // RB_DEV)
    routes_turns = jax.random.permutation(jax.random.fold_in(streams_of[1], 3), RB_TOTAL // RB_DEV)
    routes = jax.vmap(lambda own, number: deal_out(jax.random.fold_in(streams_of[1], 2), own, number, RB_DEV, DEVICES, 2, CAP, 2))(routes_keys, routes_turns).reshape((RB_TOTAL, 2))
    dam_field = centred(streams_of[2], (DNODE_TOTAL, 3 * SAMPLES), 1.0, 6.0, ((0, 128),))
    conn_free = with_ends(jax.random.randint(streams_of[3], (ELEM_TOTAL, NODES), 0, DEVICES * CAP), jax.random.fold_in(streams_of[3], 1), 0, (DEVICES * CAP) - 1).astype(jnp.int32)
    conn_dam = with_ends(jax.random.randint(streams_of[4], (ELEM_TOTAL, NODES), 0, DNODE_DEV), jax.random.fold_in(streams_of[4], 1), 0, DNODE_DEV - 1).astype(jnp.int32)
    stiff_ref = centred(streams_of[5], (3 * NODES, 3 * NODES), (3 * NODES) ** -0.5, 0.4375)
    stiff_coef = jnp.clip(jnp.exp(math.log(1.0) - 1.3862944 * jax.random.uniform(streams_of[6], (ELEM_TOTAL,), jnp.float32) ** steps_of(streams_of[6], (ELEM_TOTAL,), ((0, 128),), -0.2, 0.2)), 0.25, 1.0)
    mass_coef = jnp.clip(jnp.exp(math.log(0.1) - 1.609438 * jax.random.uniform(streams_of[7], (ELEM_TOTAL,), jnp.float32) ** steps_of(streams_of[7], (ELEM_TOTAL,), ((0, 128),), -0.2, 0.2)), 0.02, 0.1)
    reg_step = jnp.clip(jnp.exp(math.log(0.2) - 1.3862944 * jax.random.uniform(streams_of[8], (RB_TOTAL,), jnp.float32) ** steps_of(streams_of[8], (RB_TOTAL,), ((0, 128),), -0.2, 0.2)), 0.05, 0.2)
    dam_step = jnp.clip(jnp.exp(math.log(0.2) - 1.3862944 * jax.random.uniform(streams_of[9], (DNODE_TOTAL,), jnp.float32) ** steps_of(streams_of[9], (DNODE_TOTAL,), ((0, 128),), -0.2, 0.2)), 0.05, 0.2)
    return {"history": history, "routes": routes, "dam_field": dam_field, "conn_free": conn_free, "conn_dam": conn_dam, "stiff_ref": stiff_ref, "stiff_coef": stiff_coef, "mass_coef": mass_coef, "reg_step": reg_step, "dam_step": dam_step}


def element_force(u_free, u_dam, stiff_ref, stiff_part, mass_part):
    count, nodes, row_width = u_free.shape
    samples = row_width // 3
    free_mat = u_free.astype(jnp.float32).reshape(count, nodes * 3, samples)
    dam_mat = u_dam.astype(jnp.float32).reshape(count, nodes * 3, samples)
    stiff_full = stiff_ref.astype(jnp.float32)
    stiff_sum = jnp.einsum("ij,ejt->eit", stiff_full, free_mat) + jnp.einsum("ij,ejt->eit", stiff_full, dam_mat)
    total = free_mat + dam_mat
    padded = jnp.pad(total, ((0, 0), (0, 0), (1, 1)))
    accel = padded[:, :, 2:] - 2.0 * total + padded[:, :, :-2]
    force = stiff_part[:, None, None] * stiff_sum + mass_part[:, None, None] * accel
    return force.reshape(count, nodes, row_width)


def inverse_table(routes):
    entries = routes.reshape(DEVICES, 2 * RB_DEV).astype(jnp.int32)
    numbers = jnp.arange(DEVICES, dtype=jnp.int32)
    onehot = (entries[:, :, None] == numbers[None, None, :]).astype(jnp.int32)
    before = jnp.cumsum(onehot, axis=1) - onehot
    slot = jnp.sum(before * onehot, axis=2).astype(jnp.int32)
    source = jnp.arange(DEVICES, dtype=jnp.int32)[:, None]
    column = (source * CAP + slot).astype(jnp.int32)
    row_id = (jnp.arange(2 * RB_TOTAL, dtype=jnp.int32) // 2).reshape(DEVICES, 2 * RB_DEV)
    table = jnp.full((DEVICES, DEVICES * CAP), -1, dtype=jnp.int32)
    return table.at[entries, column].set(row_id)


def reference(history, routes, dam_field, conn_free, conn_dam, stiff_ref, stiff_coef, mass_coef, reg_step, dam_step):
    row_width = history.shape[1]
    inverse = inverse_table(routes)
    free_dev = conn_free.reshape(DEVICES, ELEM_DEV, NODES)
    dam_refs_dev = conn_dam.reshape(DEVICES, ELEM_DEV, NODES)
    stiff_dev = stiff_coef.reshape(DEVICES, ELEM_DEV)
    mass_dev = mass_coef.reshape(DEVICES, ELEM_DEV)
    damstep_dev = dam_step.reshape(DEVICES, DNODE_DEV)
    pulled = jnp.zeros((RB_TOTAL, row_width), jnp.float32)
    for round_index in range(ROUNDS):
        dam_dev = dam_field.reshape(DEVICES, DNODE_DEV, row_width)
        current = history

        def per_device(carry, pieces):
            table, free_refs, dam_refs, stiff_part, mass_part, dam_local, step_local = pieces
            targets = table[free_refs]
            live = targets >= 0
            safe = jnp.maximum(targets, 0)
            u_free = jnp.where(live[:, :, None], current[safe], jnp.zeros((), current.dtype))
            u_dam = dam_local[dam_refs]
            force = element_force(u_free, u_dam, stiff_ref, stiff_part, mass_part)
            kept = jnp.where(live[:, :, None], force, jnp.zeros((), jnp.float32))
            carry = carry.at[safe.reshape(-1)].add(kept.reshape(-1, row_width))
            dam_sum = jnp.zeros((DNODE_DEV, row_width), jnp.float32).at[dam_refs.reshape(-1)].add(force.reshape(-1, row_width))
            dam_next = (dam_local.astype(jnp.float32) - step_local[:, None] * dam_sum).astype(jnp.bfloat16)
            return carry, dam_next

        start = jnp.zeros((RB_TOTAL, row_width), jnp.float32)
        pulled, dam_stack = lax.scan(per_device, start, (inverse, free_dev, dam_refs_dev, stiff_dev, mass_dev, dam_dev, damstep_dev))
        history = (history.astype(jnp.float32) - reg_step[:, None] * pulled).astype(jnp.bfloat16)
        dam_field = dam_stack.reshape(DNODE_TOTAL, row_width)
    return (history, pulled, dam_field)
```

```python
import jax
import jax.numpy as jnp
from jax import lax
from jax.experimental import pallas as pl
from jax.experimental.pallas import tpu as pltpu
from jax.sharding import PartitionSpec as P

ROUNDS = 2
GROUP = 4


def one_hot(indices, width):
    numbers = jnp.arange(width, dtype=jnp.int32)
    return (indices.reshape(-1)[:, None] == numbers[None, :]).astype(jnp.bfloat16)


def split_three(values):
    upper = lax.optimization_barrier(values.astype(jnp.bfloat16))
    rest = values - upper.astype(jnp.float32)
    middle = lax.optimization_barrier(rest.astype(jnp.bfloat16))
    lower = (rest - middle.astype(jnp.float32)).astype(jnp.bfloat16)
    return (upper, middle, lower)


def apply_exact(selector, values, transpose):
    dims = (((0,), (0,)), ((), ())) if transpose else (((1,), (0,)), ((), ()))
    total = None
    for piece in split_three(values):
        term = lax.dot_general(selector, piece, dims, preferred_element_type=jnp.float32)
        total = term if total is None else total + term
    return total


def block_places(routes, devices, capacity):
    entries = routes.reshape(-1)
    numbers = jnp.arange(devices, dtype=jnp.int32)
    onehot = (entries[:, None] == numbers[None, :]).astype(jnp.int32)
    before = jnp.cumsum(onehot, axis=0) - onehot
    slot = jnp.sum(before * onehot, axis=1)
    return entries * capacity + slot


def carry_blocks(outgoing, devices, capacity):
    row_width = outgoing.shape[1]
    shaped = outgoing.reshape(devices, capacity, row_width)
    arrived = lax.all_to_all(shaped, ("reg", "dam"), split_axis=0, concat_axis=0, tiled=True)
    return arrived.reshape(devices * capacity, row_width)


def element_kernel(sc_ref, mc_ref, r_ref, d_ref, cf_ref, cd_ref, s2_ref, dstep_ref,
                   back_ref, dnext_ref, dsum_ref):
    f32, bf16 = jnp.float32, jnp.bfloat16
    slots = r_ref.shape[0]
    dcount = d_ref.shape[0]
    groups, width = cf_ref.shape
    nodes = width // GROUP
    samples = r_ref.shape[1] // 3
    back_ref[...] = jnp.zeros(back_ref.shape, f32)
    dsum_ref[...] = jnp.zeros(dsum_ref.shape, f32)

    def body(g, carry):
        cf = cf_ref[pl.ds(g, 1), :]
        cd = cd_ref[pl.ds(g, 1), :]
        ohtf = (lax.broadcasted_iota(jnp.int32, (slots, width), 0) == cf).astype(f32)
        ohtd = (lax.broadcasted_iota(jnp.int32, (dcount, width), 0) == cd).astype(f32)
        ohf = jnp.transpose(ohtf).astype(bf16)
        ohd = jnp.transpose(ohtd).astype(bf16)
        uf = jnp.dot(ohf, r_ref[...], preferred_element_type=f32).astype(bf16)
        ud = jnp.dot(ohd, d_ref[...], preferred_element_type=f32).astype(bf16)
        forces = []
        for k in range(GROUP):
            e = g * GROUP + k
            lo_row, hi_row = k * nodes, (k + 1) * nodes
            wf = jnp.concatenate(
                [uf[lo_row:hi_row, c * samples:(c + 1) * samples] for c in range(3)], axis=0)
            wd = jnp.concatenate(
                [ud[lo_row:hi_row, c * samples:(c + 1) * samples] for c in range(3)], axis=0)
            x = jnp.concatenate([wf, wd], axis=0)
            ss = jnp.dot(s2_ref[...], x, preferred_element_type=f32)
            tot = wf.astype(f32) + wd.astype(f32)
            lane = lax.broadcasted_iota(jnp.int32, tot.shape, 1)
            prev = jnp.where(lane == 0, 0.0, pltpu.roll(tot, 1, 1))
            nxt = jnp.where(lane == samples - 1, 0.0, pltpu.roll(tot, samples - 1, 1))
            accel = (nxt - 2.0 * tot) + prev
            f = sc_ref[e] * ss + mc_ref[e] * accel
            forces.append(
                jnp.concatenate([f[c * nodes:(c + 1) * nodes, :] for c in range(3)], axis=1))
        fg = jnp.concatenate(forces, axis=0)
        hi = fg.astype(bf16)
        lo = (fg - hi.astype(f32)).astype(bf16)
        ohtf_b = ohtf.astype(bf16)
        ohtd_b = ohtd.astype(bf16)
        back_ref[...] += (jnp.dot(ohtf_b, hi, preferred_element_type=f32)
                          + jnp.dot(ohtf_b, lo, preferred_element_type=f32))
        dsum_ref[...] += (jnp.dot(ohtd_b, hi, preferred_element_type=f32)
                          + jnp.dot(ohtd_b, lo, preferred_element_type=f32))
        return carry

    lax.fori_loop(0, groups, body, 0)
    dnext_ref[...] = (d_ref[...].astype(f32) - dstep_ref[...] * dsum_ref[...]).astype(bf16)


def element_work(received, dam_field, conn_rows, dam_rows, s2, stiff_coef, mass_coef, dam_col):
    smem = pl.BlockSpec(memory_space=pltpu.SMEM)
    vmem = pl.BlockSpec(memory_space=pltpu.VMEM)
    return pl.pallas_call(
        element_kernel,
        out_shape=(jax.ShapeDtypeStruct(received.shape, jnp.float32),
                   jax.ShapeDtypeStruct(dam_field.shape, jnp.bfloat16)),
        in_specs=[smem, smem] + [vmem] * 6,
        out_specs=(vmem, vmem),
        scratch_shapes=[pltpu.VMEM(dam_field.shape, jnp.float32)],
    )(stiff_coef, mass_coef, received, dam_field, conn_rows, dam_rows, s2, dam_col)


def shards(history, routes, dam_field, conn_free, conn_dam, stiff_ref, stiff_coef,
           mass_coef, reg_step, dam_step):
    devices = lax.axis_size(("reg", "dam"))
    row_count, row_width = history.shape
    capacity = 4 * row_count // devices
    nodes = conn_free.shape[1]
    order = jnp.arange(3 * nodes)
    perm = (order % nodes) * 3 + order // nodes
    s_perm = stiff_ref[perm][:, perm]
    s2 = jnp.concatenate([s_perm, s_perm], axis=1)
    conn_rows = conn_free.reshape(-1, GROUP * nodes)
    dam_rows = conn_dam.reshape(-1, GROUP * nodes)
    dam_col = dam_step.reshape(-1, 1)
    places = block_places(routes, devices, capacity)
    place_select = one_hot(places, devices * capacity)
    pair_select = place_select.reshape(row_count, 2, devices * capacity).sum(axis=1)
    pulled = jnp.zeros((row_count, row_width), jnp.float32)
    for round_index in range(ROUNDS):
        spread = jnp.repeat(history, 2, axis=0)
        outgoing = lax.dot_general(
            place_select, spread, (((0,), (0,)), ((), ())), preferred_element_type=jnp.float32
        ).astype(jnp.bfloat16)
        received = carry_blocks(outgoing, devices, capacity)
        backward_sums, dam_field = element_work(
            received, dam_field, conn_rows, dam_rows, s2, stiff_coef, mass_coef, dam_col)
        returned = carry_blocks(backward_sums, devices, capacity)
        pulled = apply_exact(pair_select, returned, False)
        history = (history.astype(jnp.float32) - reg_step[:, None] * pulled).astype(jnp.bfloat16)
    return (history, pulled, dam_field)


def solution(mesh):
    in_specs = (
        P(("reg", "dam"), None),
        P(("reg", "dam"), None),
        P(("reg", "dam"), None),
        P(("reg", "dam"), None),
        P(("reg", "dam"), None),
        P(),
        P(("reg", "dam")),
        P(("reg", "dam")),
        P(("reg", "dam")),
        P(("reg", "dam")),
    )
    out_specs = (P(("reg", "dam"), None), P(("reg", "dam"), None), P(("reg", "dam"), None))
    return jax.shard_map(shards, mesh=mesh, in_specs=in_specs, out_specs=out_specs, check_vma=False)
```

```python
import functools

import jax
import jax.numpy as jnp
from jax import lax
from jax.experimental import pallas as pl
from jax.experimental.pallas import tpu as pltpu
from jax.sharding import PartitionSpec as P

ROUNDS = 2
GROUP = 4


def one_hot(indices, width):
    numbers = jnp.arange(width, dtype=jnp.int32)
    return (indices.reshape(-1)[:, None] == numbers[None, :]).astype(jnp.bfloat16)


def split_three(values):
    upper = lax.optimization_barrier(values.astype(jnp.bfloat16))
    rest = values - upper.astype(jnp.float32)
    middle = lax.optimization_barrier(rest.astype(jnp.bfloat16))
    lower = (rest - middle.astype(jnp.float32)).astype(jnp.bfloat16)
    return (upper, middle, lower)


def apply_exact(selector, values, transpose):
    dims = (((0,), (0,)), ((), ())) if transpose else (((1,), (0,)), ((), ()))
    total = None
    for piece in split_three(values):
        term = lax.dot_general(selector, piece, dims, preferred_element_type=jnp.float32)
        total = term if total is None else total + term
    return total


def block_places(routes, devices, capacity):
    entries = routes.reshape(-1)
    numbers = jnp.arange(devices, dtype=jnp.int32)
    onehot = (entries[:, None] == numbers[None, :]).astype(jnp.int32)
    before = jnp.cumsum(onehot, axis=0) - onehot
    slot = jnp.sum(before * onehot, axis=1)
    return entries * capacity + slot


def exchange_kernel(n, ndam, x_ref, o_ref, send_sem, recv_sem, local_sem):
    me = lax.axis_index("reg") * ndam + lax.axis_index("dam")
    mesh_id = pl.DeviceIdType.MESH
    barrier = pltpu.get_barrier_semaphore()

    def greet(step, carry):
        peer = lax.rem(me + step, n)
        pl.semaphore_signal(barrier, 1, device_id=(peer // ndam, peer % ndam),
                            device_id_type=mesh_id)
        return carry

    lax.fori_loop(1, n, greet, 0)
    pl.semaphore_wait(barrier, n - 1)

    def send(step, carry):
        peer = lax.rem(me + step, n)
        pltpu.make_async_remote_copy(
            src_ref=x_ref.at[peer],
            dst_ref=o_ref.at[me],
            send_sem=send_sem,
            recv_sem=recv_sem,
            device_id=(peer // ndam, peer % ndam),
            device_id_type=mesh_id,
        ).start()
        return carry

    own = pltpu.make_async_copy(x_ref.at[me], o_ref.at[me], local_sem)
    own.start()
    lax.fori_loop(1, n, send, 0)
    everything = pltpu.make_async_remote_copy(
        src_ref=x_ref.at[pl.ds(0, n - 1)],
        dst_ref=o_ref.at[pl.ds(0, n - 1)],
        send_sem=send_sem,
        recv_sem=recv_sem,
        device_id=(me // ndam, me % ndam),
        device_id_type=mesh_id,
    )
    everything.wait_send()
    everything.wait_recv()
    own.wait()


def carry_blocks(outgoing, devices, capacity):
    ndam = lax.axis_size("dam")
    row_width = outgoing.shape[1]
    shaped = outgoing.reshape(devices, capacity, row_width)
    anywhere = pl.BlockSpec(memory_space=pl.ANY)
    kernel_id = 1 if outgoing.dtype == jnp.float32 else 0
    arrived = pl.pallas_call(
        functools.partial(exchange_kernel, devices, ndam),
        out_shape=jax.ShapeDtypeStruct(shaped.shape, shaped.dtype),
        in_specs=[anywhere],
        out_specs=anywhere,
        scratch_shapes=[pltpu.SemaphoreType.DMA] * 3,
        compiler_params=pltpu.CompilerParams(collective_id=kernel_id, has_side_effects=True),
    )(shaped)
    return arrived.reshape(devices * capacity, row_width)


def element_kernel(sc_ref, mc_ref, r_ref, d_ref, cf_ref, cd_ref, s2_ref, dstep_ref,
                   back_ref, dnext_ref, dsum_ref):
    f32, bf16 = jnp.float32, jnp.bfloat16
    slots = r_ref.shape[0]
    dcount = d_ref.shape[0]
    groups, width = cf_ref.shape
    nodes = width // GROUP
    samples = r_ref.shape[1] // 3
    back_ref[...] = jnp.zeros(back_ref.shape, f32)
    dsum_ref[...] = jnp.zeros(dsum_ref.shape, f32)

    def body(g, carry):
        cf = cf_ref[pl.ds(g, 1), :]
        cd = cd_ref[pl.ds(g, 1), :]
        ohtf = (lax.broadcasted_iota(jnp.int32, (slots, width), 0) == cf).astype(f32)
        ohtd = (lax.broadcasted_iota(jnp.int32, (dcount, width), 0) == cd).astype(f32)
        ohf = jnp.transpose(ohtf).astype(bf16)
        ohd = jnp.transpose(ohtd).astype(bf16)
        uf = jnp.dot(ohf, r_ref[...], preferred_element_type=f32).astype(bf16)
        ud = jnp.dot(ohd, d_ref[...], preferred_element_type=f32).astype(bf16)
        forces = []
        for k in range(GROUP):
            e = g * GROUP + k
            lo_row, hi_row = k * nodes, (k + 1) * nodes
            wf = jnp.concatenate(
                [uf[lo_row:hi_row, c * samples:(c + 1) * samples] for c in range(3)], axis=0)
            wd = jnp.concatenate(
                [ud[lo_row:hi_row, c * samples:(c + 1) * samples] for c in range(3)], axis=0)
            x = jnp.concatenate([wf, wd], axis=0)
            ss = jnp.dot(s2_ref[...], x, preferred_element_type=f32)
            tot = wf.astype(f32) + wd.astype(f32)
            lane = lax.broadcasted_iota(jnp.int32, tot.shape, 1)
            prev = jnp.where(lane == 0, 0.0, pltpu.roll(tot, 1, 1))
            nxt = jnp.where(lane == samples - 1, 0.0, pltpu.roll(tot, samples - 1, 1))
            accel = (nxt - 2.0 * tot) + prev
            f = sc_ref[e] * ss + mc_ref[e] * accel
            forces.append(
                jnp.concatenate([f[c * nodes:(c + 1) * nodes, :] for c in range(3)], axis=1))
        fg = jnp.concatenate(forces, axis=0)
        hi = fg.astype(bf16)
        lo = (fg - hi.astype(f32)).astype(bf16)
        ohtf_b = ohtf.astype(bf16)
        ohtd_b = ohtd.astype(bf16)
        back_ref[...] += (jnp.dot(ohtf_b, hi, preferred_element_type=f32)
                          + jnp.dot(ohtf_b, lo, preferred_element_type=f32))
        dsum_ref[...] += (jnp.dot(ohtd_b, hi, preferred_element_type=f32)
                          + jnp.dot(ohtd_b, lo, preferred_element_type=f32))
        return carry

    lax.fori_loop(0, groups, body, 0)
    dnext_ref[...] = (d_ref[...].astype(f32) - dstep_ref[...] * dsum_ref[...]).astype(bf16)


def element_work(received, dam_field, conn_rows, dam_rows, s2, stiff_coef, mass_coef, dam_col):
    smem = pl.BlockSpec(memory_space=pltpu.SMEM)
    vmem = pl.BlockSpec(memory_space=pltpu.VMEM)
    return pl.pallas_call(
        element_kernel,
        out_shape=(jax.ShapeDtypeStruct(received.shape, jnp.float32),
                   jax.ShapeDtypeStruct(dam_field.shape, jnp.bfloat16)),
        in_specs=[smem, smem] + [vmem] * 6,
        out_specs=(vmem, vmem),
        scratch_shapes=[pltpu.VMEM(dam_field.shape, jnp.float32)],
    )(stiff_coef, mass_coef, received, dam_field, conn_rows, dam_rows, s2, dam_col)


def shards(history, routes, dam_field, conn_free, conn_dam, stiff_ref, stiff_coef,
           mass_coef, reg_step, dam_step):
    devices = lax.axis_size(("reg", "dam"))
    row_count, row_width = history.shape
    capacity = 4 * row_count // devices
    nodes = conn_free.shape[1]
    order = jnp.arange(3 * nodes)
    perm = (order % nodes) * 3 + order // nodes
    s_perm = stiff_ref[perm][:, perm]
    s2 = jnp.concatenate([s_perm, s_perm], axis=1)
    conn_rows = conn_free.reshape(-1, GROUP * nodes)
    dam_rows = conn_dam.reshape(-1, GROUP * nodes)
    dam_col = dam_step.reshape(-1, 1)
    places = block_places(routes, devices, capacity)
    place_select = one_hot(places, devices * capacity)
    pair_select = place_select.reshape(row_count, 2, devices * capacity).sum(axis=1)
    pulled = jnp.zeros((row_count, row_width), jnp.float32)
    for round_index in range(ROUNDS):
        spread = jnp.repeat(history, 2, axis=0)
        outgoing = lax.dot_general(
            place_select, spread, (((0,), (0,)), ((), ())), preferred_element_type=jnp.float32
        ).astype(jnp.bfloat16)
        received = carry_blocks(outgoing, devices, capacity)
        backward_sums, dam_field = element_work(
            received, dam_field, conn_rows, dam_rows, s2, stiff_coef, mass_coef, dam_col)
        returned = carry_blocks(backward_sums, devices, capacity)
        pulled = apply_exact(pair_select, returned, False)
        history = (history.astype(jnp.float32) - reg_step[:, None] * pulled).astype(jnp.bfloat16)
    return (history, pulled, dam_field)


def solution(mesh):
    in_specs = (
        P(("reg", "dam"), None),
        P(("reg", "dam"), None),
        P(("reg", "dam"), None),
        P(("reg", "dam"), None),
        P(("reg", "dam"), None),
        P(),
        P(("reg", "dam")),
        P(("reg", "dam")),
        P(("reg", "dam")),
        P(("reg", "dam")),
    )
    out_specs = (P(("reg", "dam"), None), P(("reg", "dam"), None), P(("reg", "dam"), None))
    return jax.shard_map(shards, mesh=mesh, in_specs=in_specs, out_specs=out_specs, check_vma=False)
```

```python
import functools

import jax
import jax.numpy as jnp
from jax import lax
from jax.experimental import pallas as pl
from jax.experimental.pallas import tpu as pltpu
from jax.sharding import PartitionSpec as P

ROUNDS = 2
GROUP = 4


def one_hot(indices, width):
    numbers = jnp.arange(width, dtype=jnp.int32)
    return (indices.reshape(-1)[:, None] == numbers[None, :]).astype(jnp.bfloat16)


def block_places(routes, devices, capacity):
    entries = routes.reshape(-1)
    numbers = jnp.arange(devices, dtype=jnp.int32)
    onehot = (entries[:, None] == numbers[None, :]).astype(jnp.int32)
    before = jnp.cumsum(onehot, axis=0) - onehot
    slot = jnp.sum(before * onehot, axis=1)
    return entries * capacity + slot


def coupling_kernel(n, ndam, sc_ref, mc_ref, hist_ref, dam_ref, cf_ref, cd_ref, sp_ref,
                    dstep_ref, rstep_ref, qt_ref, q_ref,
                    hist_out, pulled_out, dam_out,
                    land_f0, land_f1, land_b0, land_b1,
                    stage_f, stage_b, landv_f, landv_b,
                    recv, ud_buf, ssd_buf, hi_buf, lo_buf, back, dsum, ret, sems):
    f32, bf16 = jnp.float32, jnp.bfloat16
    mesh_id = pl.DeviceIdType.MESH
    me = lax.axis_index("reg") * ndam + lax.axis_index("dam")
    slots = recv.shape[0]
    dcount = dam_out.shape[0]
    groups, width = cf_ref.shape
    nodes = width // GROUP
    samples = recv.shape[1] // 3
    lands_f, lands_b = (land_f0, land_f1), (land_b0, land_b1)
    blocks = stage_f.shape

    barrier = pltpu.get_barrier_semaphore()

    def greet(step, carry):
        peer = lax.rem(me + step, n)
        pl.semaphore_signal(barrier, 1, device_id=(peer // ndam, peer % ndam),
                            device_id_type=mesh_id)
        return carry

    lax.fori_loop(1, n, greet, 0)
    pl.semaphore_wait(barrier, n - 1)

    def local_copy(src, dst):
        cp = pltpu.make_async_copy(src, dst, sems.at[0])
        cp.start()
        cp.wait()

    def start_exchange(stage, land, base):
        own = pltpu.make_async_copy(stage.at[me], land.at[me], sems.at[base + 2])
        own.start()

        def send(step, carry):
            peer = lax.rem(me + step, n)
            pltpu.make_async_remote_copy(
                src_ref=stage.at[peer],
                dst_ref=land.at[me],
                send_sem=sems.at[base],
                recv_sem=sems.at[base + 1],
                device_id=(peer // ndam, peer % ndam),
                device_id_type=mesh_id,
            ).start()
            return carry

        lax.fori_loop(1, n, send, 0)
        return own

    def finish_exchange(stage, land, base, own):
        everything = pltpu.make_async_remote_copy(
            src_ref=stage.at[pl.ds(0, n - 1)],
            dst_ref=land.at[pl.ds(0, n - 1)],
            send_sem=sems.at[base],
            recv_sem=sems.at[base + 1],
            device_id=(me // ndam, me % ndam),
            device_id_type=mesh_id,
        )
        everything.wait_send()
        everything.wait_recv()
        own.wait()

    def dam_select(g):
        cd = cd_ref[pl.ds(g, 1), :]
        return (lax.broadcasted_iota(jnp.int32, (dcount, width), 0) == cd).astype(f32)

    def free_select(g):
        cf = cf_ref[pl.ds(g, 1), :]
        return (lax.broadcasted_iota(jnp.int32, (slots, width), 0) == cf).astype(f32)

    def node_major(u, k):
        lo_row, hi_row = k * nodes, (k + 1) * nodes
        return jnp.concatenate(
            [u[lo_row:hi_row, c * samples:(c + 1) * samples] for c in range(3)], axis=0)

    def dam_side(g, carry):
        ohd = jnp.transpose(dam_select(g)).astype(bf16)
        ud = jnp.dot(ohd, dam_out[...], preferred_element_type=f32).astype(bf16)
        rows = pl.ds(pl.multiple_of(g * width, width), width)
        ud_buf[rows, :] = ud
        for k in range(GROUP):
            ssd_buf[g * GROUP + k] = jnp.dot(sp_ref[...], node_major(ud, k),
                                             preferred_element_type=f32)
        return carry

    def free_side(g, carry):
        ohtf = free_select(g)
        ohf = jnp.transpose(ohtf).astype(bf16)
        uf = jnp.dot(ohf, recv[...], preferred_element_type=f32).astype(bf16)
        rows = pl.ds(pl.multiple_of(g * width, width), width)
        ud = ud_buf[rows, :]
        forces = []
        for k in range(GROUP):
            e = g * GROUP + k
            wf = node_major(uf, k)
            wd = node_major(ud, k)
            ss = ssd_buf[e] + jnp.dot(sp_ref[...], wf, preferred_element_type=f32)
            tot = wf.astype(f32) + wd.astype(f32)
            lane = lax.broadcasted_iota(jnp.int32, tot.shape, 1)
            prev = jnp.where(lane == 0, 0.0, pltpu.roll(tot, 1, 1))
            nxt = jnp.where(lane == samples - 1, 0.0, pltpu.roll(tot, samples - 1, 1))
            accel = (nxt - 2.0 * tot) + prev
            f = sc_ref[e] * ss + mc_ref[e] * accel
            forces.append(
                jnp.concatenate([f[c * nodes:(c + 1) * nodes, :] for c in range(3)], axis=1))
        fg = jnp.concatenate(forces, axis=0)
        hi = fg.astype(bf16)
        lo = (fg - hi.astype(f32)).astype(bf16)
        hi_buf[rows, :] = hi
        lo_buf[rows, :] = lo
        sel = ohtf.astype(bf16)
        back[...] += (jnp.dot(sel, hi, preferred_element_type=f32)
                      + jnp.dot(sel, lo, preferred_element_type=f32))
        return carry

    def dam_scatter(g, carry):
        sel = dam_select(g).astype(bf16)
        rows = pl.ds(pl.multiple_of(g * width, width), width)
        dsum[...] += (jnp.dot(sel, hi_buf[rows, :], preferred_element_type=f32)
                      + jnp.dot(sel, lo_buf[rows, :], preferred_element_type=f32))
        return carry

    hist_out[...] = hist_ref[...]
    dam_out[...] = dam_ref[...]
    for r in range(ROUNDS):
        base_f, base_b = 1 + 6 * r, 4 + 6 * r
        outgoing = jnp.dot(qt_ref[...], hist_out[...], preferred_element_type=f32).astype(bf16)
        stage_f[...] = outgoing.reshape(blocks)
        own_f = start_exchange(stage_f, lands_f[r], base_f)
        lax.fori_loop(0, groups, dam_side, 0)
        finish_exchange(stage_f, lands_f[r], base_f, own_f)
        local_copy(lands_f[r], landv_f)
        recv[...] = landv_f[...].reshape(recv.shape)

        back[...] = jnp.zeros(back.shape, f32)
        lax.fori_loop(0, groups, free_side, 0)
        stage_b[...] = back[...].reshape(blocks)
        own_b = start_exchange(stage_b, lands_b[r], base_b)
        dsum[...] = jnp.zeros(dsum.shape, f32)
        lax.fori_loop(0, groups, dam_scatter, 0)
        dam_out[...] = (dam_out[...].astype(f32) - dstep_ref[...] * dsum[...]).astype(bf16)
        finish_exchange(stage_b, lands_b[r], base_b, own_b)
        local_copy(lands_b[r], landv_b)
        ret[...] = landv_b[...].reshape(ret.shape)

        returned = ret[...]
        ret_hi = returned.astype(bf16)
        ret_lo = (returned - ret_hi.astype(f32)).astype(bf16)
        pulled = (jnp.dot(q_ref[...], ret_hi, preferred_element_type=f32)
                  + jnp.dot(q_ref[...], ret_lo, preferred_element_type=f32))
        hist_out[...] = (hist_out[...].astype(f32) - rstep_ref[...] * pulled).astype(bf16)
        if r == ROUNDS - 1:
            pulled_out[...] = pulled


def shards(history, routes, dam_field, conn_free, conn_dam, stiff_ref, stiff_coef,
           mass_coef, reg_step, dam_step):
    devices = lax.axis_size(("reg", "dam"))
    ndam = lax.axis_size("dam")
    row_count, row_width = history.shape
    capacity = 4 * row_count // devices
    slots = devices * capacity
    nodes = conn_free.shape[1]
    samples = row_width // 3
    order = jnp.arange(3 * nodes)
    perm = (order % nodes) * 3 + order // nodes
    s_perm = stiff_ref[perm][:, perm]
    conn_rows = conn_free.reshape(-1, GROUP * nodes)
    dam_rows = conn_dam.reshape(-1, GROUP * nodes)
    places = block_places(routes, devices, capacity)
    pair_select = one_hot(places, slots).reshape(row_count, 2, slots).sum(axis=1)
    smem = pl.BlockSpec(memory_space=pltpu.SMEM)
    vmem = pl.BlockSpec(memory_space=pltpu.VMEM)
    anywhere = pl.BlockSpec(memory_space=pl.ANY)
    elements = conn_free.shape[0]
    hbm_f = jax.ShapeDtypeStruct((devices, capacity, row_width), jnp.bfloat16)
    hbm_b = jax.ShapeDtypeStruct((devices, capacity, row_width), jnp.float32)
    outs = pl.pallas_call(
        functools.partial(coupling_kernel, devices, ndam),
        out_shape=(
            jax.ShapeDtypeStruct(history.shape, jnp.bfloat16),
            jax.ShapeDtypeStruct(history.shape, jnp.float32),
            jax.ShapeDtypeStruct(dam_field.shape, jnp.bfloat16),
            hbm_f, hbm_f, hbm_b, hbm_b,
        ),
        in_specs=[smem, smem] + [vmem] * 9,
        out_specs=(vmem, vmem, vmem) + (anywhere,) * 4,
        scratch_shapes=[
            pltpu.VMEM(hbm_f.shape, jnp.bfloat16),
            pltpu.VMEM(hbm_b.shape, jnp.float32),
            pltpu.VMEM(hbm_f.shape, jnp.bfloat16),
            pltpu.VMEM(hbm_b.shape, jnp.float32),
            pltpu.VMEM((slots, row_width), jnp.bfloat16),
            pltpu.VMEM((elements * nodes, row_width), jnp.bfloat16),
            pltpu.VMEM((elements, 3 * nodes, samples), jnp.float32),
            pltpu.VMEM((elements * nodes, row_width), jnp.bfloat16),
            pltpu.VMEM((elements * nodes, row_width), jnp.bfloat16),
            pltpu.VMEM((slots, row_width), jnp.float32),
            pltpu.VMEM(dam_field.shape, jnp.float32),
            pltpu.VMEM((slots, row_width), jnp.float32),
            pltpu.SemaphoreType.DMA((1 + 6 * ROUNDS,)),
        ],
        compiler_params=pltpu.CompilerParams(
            collective_id=0, has_side_effects=True, vmem_limit_bytes=48 * 1024 * 1024),
    )(stiff_coef, mass_coef, history, dam_field, conn_rows, dam_rows, s_perm,
      dam_step.reshape(-1, 1), reg_step.reshape(-1, 1), jnp.transpose(pair_select), pair_select)
    return (outs[0], outs[1], outs[2])


def solution(mesh):
    in_specs = (
        P(("reg", "dam"), None),
        P(("reg", "dam"), None),
        P(("reg", "dam"), None),
        P(("reg", "dam"), None),
        P(("reg", "dam"), None),
        P(),
        P(("reg", "dam")),
        P(("reg", "dam")),
        P(("reg", "dam")),
        P(("reg", "dam")),
    )
    out_specs = (P(("reg", "dam"), None), P(("reg", "dam"), None), P(("reg", "dam"), None))
    return jax.shard_map(shards, mesh=mesh, in_specs=in_specs, out_specs=out_specs, check_vma=False)
```

```python
import functools

import jax
import jax.numpy as jnp
from jax import lax
from jax.experimental import pallas as pl
from jax.experimental.pallas import tpu as pltpu
from jax.sharding import PartitionSpec as P

ROUNDS = 2
GROUP = 4


def one_hot(indices, width):
    numbers = jnp.arange(width, dtype=jnp.int32)
    return (indices.reshape(-1)[:, None] == numbers[None, :]).astype(jnp.bfloat16)


def block_places(routes, devices, capacity):
    entries = routes.reshape(-1)
    numbers = jnp.arange(devices, dtype=jnp.int32)
    onehot = (entries[:, None] == numbers[None, :]).astype(jnp.int32)
    before = jnp.cumsum(onehot, axis=0) - onehot
    slot = jnp.sum(before * onehot, axis=1)
    return entries * capacity + slot


def coupling_kernel(n, ndam, sc_ref, mc_ref, hist_ref, dam_ref, cf_ref, cd_ref, sp_ref,
                    dstep_ref, rstep_ref, qt_ref, q_ref,
                    hist_out, pulled_out, dam_out,
                    land_f0, land_f1, land_b0, land_b1,
                    stage_f, stage_b, landv_f, landv_b,
                    recv, ud_buf, ssd_buf, hi_buf, lo_buf, back, dsum, ret,
                    ohf_buf, ohd_buf, ohtf_buf, ohtd_buf, sems):
    f32, bf16 = jnp.float32, jnp.bfloat16
    mesh_id = pl.DeviceIdType.MESH
    me = lax.axis_index("reg") * ndam + lax.axis_index("dam")
    slots = recv.shape[0]
    dcount = dam_out.shape[0]
    groups, width = cf_ref.shape
    nodes = width // GROUP
    samples = recv.shape[1] // 3
    lands_f, lands_b = (land_f0, land_f1), (land_b0, land_b1)
    blocks = stage_f.shape

    barrier = pltpu.get_barrier_semaphore()

    def greet(step, carry):
        peer = lax.rem(me + step, n)
        pl.semaphore_signal(barrier, 1, device_id=(peer // ndam, peer % ndam),
                            device_id_type=mesh_id)
        return carry

    lax.fori_loop(1, n, greet, 0)

    def build_selectors(g, carry):
        cf = cf_ref[pl.ds(g, 1), :]
        cd = cd_ref[pl.ds(g, 1), :]
        ohtf = (lax.broadcasted_iota(jnp.int32, (slots, width), 0) == cf).astype(f32)
        ohtd = (lax.broadcasted_iota(jnp.int32, (dcount, width), 0) == cd).astype(f32)
        ohtf_buf[g] = ohtf.astype(bf16)
        ohtd_buf[g] = ohtd.astype(bf16)
        ohf_buf[g] = jnp.transpose(ohtf).astype(bf16)
        ohd_buf[g] = jnp.transpose(ohtd).astype(bf16)
        return carry

    lax.fori_loop(0, groups, build_selectors, 0)
    pl.semaphore_wait(barrier, n - 1)

    def local_copy(src, dst):
        cp = pltpu.make_async_copy(src, dst, sems.at[0])
        cp.start()
        cp.wait()

    def start_exchange(stage, land, base):
        own = pltpu.make_async_copy(stage.at[me], land.at[me], sems.at[base + 2])
        own.start()

        def send(step, carry):
            peer = lax.rem(me + step, n)
            pltpu.make_async_remote_copy(
                src_ref=stage.at[peer],
                dst_ref=land.at[me],
                send_sem=sems.at[base],
                recv_sem=sems.at[base + 1],
                device_id=(peer // ndam, peer % ndam),
                device_id_type=mesh_id,
            ).start()
            return carry

        lax.fori_loop(1, n, send, 0)
        return own

    def finish_exchange(stage, land, base, own):
        everything = pltpu.make_async_remote_copy(
            src_ref=stage.at[pl.ds(0, n - 1)],
            dst_ref=land.at[pl.ds(0, n - 1)],
            send_sem=sems.at[base],
            recv_sem=sems.at[base + 1],
            device_id=(me // ndam, me % ndam),
            device_id_type=mesh_id,
        )
        everything.wait_send()
        everything.wait_recv()
        own.wait()

    def node_major(u, k):
        lo_row, hi_row = k * nodes, (k + 1) * nodes
        return jnp.concatenate(
            [u[lo_row:hi_row, c * samples:(c + 1) * samples] for c in range(3)], axis=0)

    def dam_side(g, carry):
        ud = jnp.dot(ohd_buf[g], dam_out[...], preferred_element_type=f32).astype(bf16)
        rows = pl.ds(pl.multiple_of(g * width, width), width)
        ud_buf[rows, :] = ud
        for k in range(GROUP):
            ssd_buf[g * GROUP + k] = jnp.dot(sp_ref[...], node_major(ud, k),
                                             preferred_element_type=f32)
        return carry

    def free_side(g, carry):
        uf = jnp.dot(ohf_buf[g], recv[...], preferred_element_type=f32).astype(bf16)
        rows = pl.ds(pl.multiple_of(g * width, width), width)
        ud = ud_buf[rows, :]
        forces = []
        for k in range(GROUP):
            e = g * GROUP + k
            wf = node_major(uf, k)
            wd = node_major(ud, k)
            ss = ssd_buf[e] + jnp.dot(sp_ref[...], wf, preferred_element_type=f32)
            tot = wf.astype(f32) + wd.astype(f32)
            lane = lax.broadcasted_iota(jnp.int32, tot.shape, 1)
            prev = jnp.where(lane == 0, 0.0, pltpu.roll(tot, 1, 1))
            nxt = jnp.where(lane == samples - 1, 0.0, pltpu.roll(tot, samples - 1, 1))
            accel = (nxt - 2.0 * tot) + prev
            f = sc_ref[e] * ss + mc_ref[e] * accel
            forces.append(
                jnp.concatenate([f[c * nodes:(c + 1) * nodes, :] for c in range(3)], axis=1))
        fg = jnp.concatenate(forces, axis=0)
        hi = fg.astype(bf16)
        lo = (fg - hi.astype(f32)).astype(bf16)
        hi_buf[rows, :] = hi
        lo_buf[rows, :] = lo
        both = jnp.dot(ohtf_buf[g], jnp.concatenate([hi, lo], axis=1),
                       preferred_element_type=f32)
        back[...] += both[:, :3 * samples] + both[:, 3 * samples:]
        return carry

    def dam_scatter(g, carry):
        rows = pl.ds(pl.multiple_of(g * width, width), width)
        both = jnp.dot(ohtd_buf[g], jnp.concatenate([hi_buf[rows, :], lo_buf[rows, :]], axis=1),
                       preferred_element_type=f32)
        dsum[...] += both[:, :3 * samples] + both[:, 3 * samples:]
        return carry

    hist_out[...] = hist_ref[...]
    dam_out[...] = dam_ref[...]
    for r in range(ROUNDS):
        base_f, base_b = 1 + 6 * r, 4 + 6 * r
        outgoing = jnp.dot(qt_ref[...], hist_out[...], preferred_element_type=f32).astype(bf16)
        stage_f[...] = outgoing.reshape(blocks)
        own_f = start_exchange(stage_f, lands_f[r], base_f)
        lax.fori_loop(0, groups, dam_side, 0)
        finish_exchange(stage_f, lands_f[r], base_f, own_f)
        local_copy(lands_f[r], landv_f)
        recv[...] = landv_f[...].reshape(recv.shape)

        back[...] = jnp.zeros(back.shape, f32)
        lax.fori_loop(0, groups, free_side, 0)
        stage_b[...] = back[...].reshape(blocks)
        own_b = start_exchange(stage_b, lands_b[r], base_b)
        dsum[...] = jnp.zeros(dsum.shape, f32)
        lax.fori_loop(0, groups, dam_scatter, 0)
        dam_out[...] = (dam_out[...].astype(f32) - dstep_ref[...] * dsum[...]).astype(bf16)
        finish_exchange(stage_b, lands_b[r], base_b, own_b)
        local_copy(lands_b[r], landv_b)
        ret[...] = landv_b[...].reshape(ret.shape)

        returned = ret[...]
        ret_hi = returned.astype(bf16)
        ret_lo = (returned - ret_hi.astype(f32)).astype(bf16)
        pulled = (jnp.dot(q_ref[...], ret_hi, preferred_element_type=f32)
                  + jnp.dot(q_ref[...], ret_lo, preferred_element_type=f32))
        hist_out[...] = (hist_out[...].astype(f32) - rstep_ref[...] * pulled).astype(bf16)
        if r == ROUNDS - 1:
            pulled_out[...] = pulled


def shards(history, routes, dam_field, conn_free, conn_dam, stiff_ref, stiff_coef,
           mass_coef, reg_step, dam_step):
    devices = lax.axis_size(("reg", "dam"))
    ndam = lax.axis_size("dam")
    row_count, row_width = history.shape
    capacity = 4 * row_count // devices
    slots = devices * capacity
    nodes = conn_free.shape[1]
    samples = row_width // 3
    order = jnp.arange(3 * nodes)
    perm = (order % nodes) * 3 + order // nodes
    s_perm = stiff_ref[perm][:, perm]
    conn_rows = conn_free.reshape(-1, GROUP * nodes)
    dam_rows = conn_dam.reshape(-1, GROUP * nodes)
    places = block_places(routes, devices, capacity)
    pair_select = one_hot(places, slots).reshape(row_count, 2, slots).sum(axis=1)
    smem = pl.BlockSpec(memory_space=pltpu.SMEM)
    vmem = pl.BlockSpec(memory_space=pltpu.VMEM)
    anywhere = pl.BlockSpec(memory_space=pl.ANY)
    elements = conn_free.shape[0]
    groups = conn_rows.shape[0]
    hbm_f = jax.ShapeDtypeStruct((devices, capacity, row_width), jnp.bfloat16)
    hbm_b = jax.ShapeDtypeStruct((devices, capacity, row_width), jnp.float32)
    outs = pl.pallas_call(
        functools.partial(coupling_kernel, devices, ndam),
        out_shape=(
            jax.ShapeDtypeStruct(history.shape, jnp.bfloat16),
            jax.ShapeDtypeStruct(history.shape, jnp.float32),
            jax.ShapeDtypeStruct(dam_field.shape, jnp.bfloat16),
            hbm_f, hbm_f, hbm_b, hbm_b,
        ),
        in_specs=[smem, smem] + [vmem] * 9,
        out_specs=(vmem, vmem, vmem) + (anywhere,) * 4,
        scratch_shapes=[
            pltpu.VMEM(hbm_f.shape, jnp.bfloat16),
            pltpu.VMEM(hbm_b.shape, jnp.float32),
            pltpu.VMEM(hbm_f.shape, jnp.bfloat16),
            pltpu.VMEM(hbm_b.shape, jnp.float32),
            pltpu.VMEM((slots, row_width), jnp.bfloat16),
            pltpu.VMEM((elements * nodes, row_width), jnp.bfloat16),
            pltpu.VMEM((elements, 3 * nodes, samples), jnp.float32),
            pltpu.VMEM((elements * nodes, row_width), jnp.bfloat16),
            pltpu.VMEM((elements * nodes, row_width), jnp.bfloat16),
            pltpu.VMEM((slots, row_width), jnp.float32),
            pltpu.VMEM(dam_field.shape, jnp.float32),
            pltpu.VMEM((slots, row_width), jnp.float32),
            pltpu.VMEM((groups, GROUP * nodes, slots), jnp.bfloat16),
            pltpu.VMEM((groups, GROUP * nodes, dam_field.shape[0]), jnp.bfloat16),
            pltpu.VMEM((groups, slots, GROUP * nodes), jnp.bfloat16),
            pltpu.VMEM((groups, dam_field.shape[0], GROUP * nodes), jnp.bfloat16),
            pltpu.SemaphoreType.DMA((1 + 6 * ROUNDS,)),
        ],
        compiler_params=pltpu.CompilerParams(
            collective_id=0, has_side_effects=True, vmem_limit_bytes=60 * 1024 * 1024),
    )(stiff_coef, mass_coef, history, dam_field, conn_rows, dam_rows, s_perm,
      dam_step.reshape(-1, 1), reg_step.reshape(-1, 1), jnp.transpose(pair_select), pair_select)
    return (outs[0], outs[1], outs[2])


def solution(mesh):
    in_specs = (
        P(("reg", "dam"), None),
        P(("reg", "dam"), None),
        P(("reg", "dam"), None),
        P(("reg", "dam"), None),
        P(("reg", "dam"), None),
        P(),
        P(("reg", "dam")),
        P(("reg", "dam")),
        P(("reg", "dam")),
        P(("reg", "dam")),
    )
    out_specs = (P(("reg", "dam"), None), P(("reg", "dam"), None), P(("reg", "dam"), None))
    return jax.shard_map(shards, mesh=mesh, in_specs=in_specs, out_specs=out_specs, check_vma=False)
```

```python
import functools

import jax
import jax.numpy as jnp
from jax import lax
from jax.experimental import pallas as pl
from jax.experimental.pallas import tpu as pltpu
from jax.sharding import PartitionSpec as P

ROUNDS = 2
GROUP = 4


def one_hot(indices, width):
    numbers = jnp.arange(width, dtype=jnp.int32)
    return (indices.reshape(-1)[:, None] == numbers[None, :]).astype(jnp.bfloat16)


def block_places(routes, devices, capacity):
    entries = routes.reshape(-1)
    numbers = jnp.arange(devices, dtype=jnp.int32)
    onehot = (entries[:, None] == numbers[None, :]).astype(jnp.int32)
    before = jnp.cumsum(onehot, axis=0) - onehot
    slot = jnp.sum(before * onehot, axis=1)
    return entries * capacity + slot


def coupling_kernel(n, ndam, sc_ref, mc_ref, hist_ref, dam_ref, cf_ref, cd_ref, stiff_ref,
                    dstep_row, rstep_row, q_ref,
                    hist_out, pulled_out, dam_out,
                    land_f0, land_f1, land_b0, land_b1,
                    stage_f, stage_b, landv_f, landv_b,
                    recv, ud_buf, ssd_buf, hi_buf, lo_buf, back, dsum, ret,
                    ohf_buf, ohd_buf, ohtf_buf, ohtd_buf, sp_ref, qt_ref, dstep_ref, rstep_ref,
                    sems):
    f32, bf16 = jnp.float32, jnp.bfloat16
    mesh_id = pl.DeviceIdType.MESH
    me = lax.axis_index("reg") * ndam + lax.axis_index("dam")
    slots = recv.shape[0]
    dcount = dam_out.shape[0]
    nodes = cf_ref.shape[1]
    width = GROUP * nodes
    groups = cf_ref.shape[0] // GROUP
    samples = recv.shape[1] // 3
    lands_f, lands_b = (land_f0, land_f1), (land_b0, land_b1)
    blocks = stage_f.shape

    barrier = pltpu.get_barrier_semaphore()

    def greet(step, carry):
        peer = lax.rem(me + step, n)
        pl.semaphore_signal(barrier, 1, device_id=(peer // ndam, peer % ndam),
                            device_id_type=mesh_id)
        return carry

    lax.fori_loop(1, n, greet, 0)

    def build_selectors(g, carry):
        for k in range(GROUP):
            lanes = slice(k * nodes, (k + 1) * nodes)
            cf = cf_ref[pl.ds(g * GROUP + k, 1), :]
            cd = cd_ref[pl.ds(g * GROUP + k, 1), :]
            ohtf_buf[g, :, lanes] = (
                lax.broadcasted_iota(jnp.int32, (slots, nodes), 0) == cf).astype(bf16)
            ohtd_buf[g, :, lanes] = (
                lax.broadcasted_iota(jnp.int32, (dcount, nodes), 0) == cd).astype(bf16)
        ohf_buf[g] = jnp.transpose(ohtf_buf[g].astype(f32)).astype(bf16)
        ohd_buf[g] = jnp.transpose(ohtd_buf[g].astype(f32)).astype(bf16)
        return carry

    lax.fori_loop(0, groups, build_selectors, 0)
    size = sp_ref.shape[0]
    across = lax.broadcasted_iota(jnp.int32, (size, size), 0)
    down = lax.broadcasted_iota(jnp.int32, (size, size), 1)
    pick_rows = (down == (across % nodes) * 3 + across // nodes).astype(bf16)
    pick_cols = (across == (down % nodes) * 3 + down // nodes).astype(bf16)
    permuted = jnp.dot(pick_rows, stiff_ref[...], preferred_element_type=f32).astype(bf16)
    sp_ref[...] = jnp.dot(permuted, pick_cols, preferred_element_type=f32).astype(bf16)
    qt_ref[...] = jnp.transpose(q_ref[...].astype(f32)).astype(bf16)
    dstep_ref[...] = jnp.transpose(
        jnp.broadcast_to(dstep_row[...], (8, dstep_row.shape[1])))[:, 0:1]
    rstep_ref[...] = jnp.transpose(
        jnp.broadcast_to(rstep_row[...], (8, rstep_row.shape[1])))[:, 0:1]
    pl.semaphore_wait(barrier, n - 1)

    def local_copy(src, dst):
        cp = pltpu.make_async_copy(src, dst, sems.at[0])
        cp.start()
        cp.wait()

    def start_exchange(stage, land, base):
        own = pltpu.make_async_copy(stage.at[me], land.at[me], sems.at[base + 2])
        own.start()

        def send(step, carry):
            peer = lax.rem(me + step, n)
            pltpu.make_async_remote_copy(
                src_ref=stage.at[peer],
                dst_ref=land.at[me],
                send_sem=sems.at[base],
                recv_sem=sems.at[base + 1],
                device_id=(peer // ndam, peer % ndam),
                device_id_type=mesh_id,
            ).start()
            return carry

        lax.fori_loop(1, n, send, 0)
        return own

    def finish_exchange(stage, land, base, own):
        everything = pltpu.make_async_remote_copy(
            src_ref=stage.at[pl.ds(0, n - 1)],
            dst_ref=land.at[pl.ds(0, n - 1)],
            send_sem=sems.at[base],
            recv_sem=sems.at[base + 1],
            device_id=(me // ndam, me % ndam),
            device_id_type=mesh_id,
        )
        everything.wait_send()
        everything.wait_recv()
        own.wait()

    def node_major(u, k):
        lo_row, hi_row = k * nodes, (k + 1) * nodes
        return jnp.concatenate(
            [u[lo_row:hi_row, c * samples:(c + 1) * samples] for c in range(3)], axis=0)

    def dam_side(g, carry):
        ud = jnp.dot(ohd_buf[g], dam_out[...], preferred_element_type=f32).astype(bf16)
        rows = pl.ds(pl.multiple_of(g * width, width), width)
        ud_buf[rows, :] = ud
        for k in range(GROUP):
            ssd_buf[g * GROUP + k] = jnp.dot(sp_ref[...], node_major(ud, k),
                                             preferred_element_type=f32)
        return carry

    def free_side(g, carry):
        uf = jnp.dot(ohf_buf[g], recv[...], preferred_element_type=f32).astype(bf16)
        rows = pl.ds(pl.multiple_of(g * width, width), width)
        ud = ud_buf[rows, :]
        forces = []
        for k in range(GROUP):
            e = g * GROUP + k
            wf = node_major(uf, k)
            wd = node_major(ud, k)
            ss = ssd_buf[e] + jnp.dot(sp_ref[...], wf, preferred_element_type=f32)
            tot = wf.astype(f32) + wd.astype(f32)
            lane = lax.broadcasted_iota(jnp.int32, tot.shape, 1)
            prev = jnp.where(lane == 0, 0.0, pltpu.roll(tot, 1, 1))
            nxt = jnp.where(lane == samples - 1, 0.0, pltpu.roll(tot, samples - 1, 1))
            accel = (nxt - 2.0 * tot) + prev
            f = sc_ref[e] * ss + mc_ref[e] * accel
            forces.append(
                jnp.concatenate([f[c * nodes:(c + 1) * nodes, :] for c in range(3)], axis=1))
        fg = jnp.concatenate(forces, axis=0)
        hi = fg.astype(bf16)
        lo = (fg - hi.astype(f32)).astype(bf16)
        hi_buf[rows, :] = hi
        lo_buf[rows, :] = lo
        both = jnp.dot(ohtf_buf[g], jnp.concatenate([hi, lo], axis=1),
                       preferred_element_type=f32)
        back[...] += both[:, :3 * samples] + both[:, 3 * samples:]
        return carry

    def dam_scatter(g, carry):
        rows = pl.ds(pl.multiple_of(g * width, width), width)
        both = jnp.dot(ohtd_buf[g], jnp.concatenate([hi_buf[rows, :], lo_buf[rows, :]], axis=1),
                       preferred_element_type=f32)
        dsum[...] += both[:, :3 * samples] + both[:, 3 * samples:]
        return carry

    hist_out[...] = hist_ref[...]
    dam_out[...] = dam_ref[...]
    for r in range(ROUNDS):
        base_f, base_b = 1 + 6 * r, 4 + 6 * r
        outgoing = jnp.dot(qt_ref[...], hist_out[...], preferred_element_type=f32).astype(bf16)
        stage_f[...] = outgoing.reshape(blocks)
        own_f = start_exchange(stage_f, lands_f[r], base_f)
        lax.fori_loop(0, groups, dam_side, 0)
        finish_exchange(stage_f, lands_f[r], base_f, own_f)
        local_copy(lands_f[r], landv_f)
        recv[...] = landv_f[...].reshape(recv.shape)

        back[...] = jnp.zeros(back.shape, f32)
        lax.fori_loop(0, groups, free_side, 0)
        stage_b[...] = back[...].reshape(blocks)
        own_b = start_exchange(stage_b, lands_b[r], base_b)
        dsum[...] = jnp.zeros(dsum.shape, f32)
        lax.fori_loop(0, groups, dam_scatter, 0)
        dam_out[...] = (dam_out[...].astype(f32) - dstep_ref[...] * dsum[...]).astype(bf16)
        finish_exchange(stage_b, lands_b[r], base_b, own_b)
        local_copy(lands_b[r], landv_b)
        ret[...] = landv_b[...].reshape(ret.shape)

        returned = ret[...]
        ret_hi = returned.astype(bf16)
        ret_lo = (returned - ret_hi.astype(f32)).astype(bf16)
        pulled = (jnp.dot(q_ref[...], ret_hi, preferred_element_type=f32)
                  + jnp.dot(q_ref[...], ret_lo, preferred_element_type=f32))
        hist_out[...] = (hist_out[...].astype(f32) - rstep_ref[...] * pulled).astype(bf16)
        if r == ROUNDS - 1:
            pulled_out[...] = pulled


def shards(history, routes, dam_field, conn_free, conn_dam, stiff_ref, stiff_coef,
           mass_coef, reg_step, dam_step):
    devices = lax.axis_size(("reg", "dam"))
    ndam = lax.axis_size("dam")
    row_count, row_width = history.shape
    capacity = 4 * row_count // devices
    slots = devices * capacity
    nodes = conn_free.shape[1]
    samples = row_width // 3
    places = block_places(routes, devices, capacity)
    pair_select = one_hot(places, slots).reshape(row_count, 2, slots).sum(axis=1)
    smem = pl.BlockSpec(memory_space=pltpu.SMEM)
    vmem = pl.BlockSpec(memory_space=pltpu.VMEM)
    anywhere = pl.BlockSpec(memory_space=pl.ANY)
    elements = conn_free.shape[0]
    groups = conn_free.shape[0] // GROUP
    hbm_f = jax.ShapeDtypeStruct((devices, capacity, row_width), jnp.bfloat16)
    hbm_b = jax.ShapeDtypeStruct((devices, capacity, row_width), jnp.float32)
    outs = pl.pallas_call(
        functools.partial(coupling_kernel, devices, ndam),
        out_shape=(
            jax.ShapeDtypeStruct(history.shape, jnp.bfloat16),
            jax.ShapeDtypeStruct(history.shape, jnp.float32),
            jax.ShapeDtypeStruct(dam_field.shape, jnp.bfloat16),
            hbm_f, hbm_f, hbm_b, hbm_b,
        ),
        in_specs=[smem, smem] + [vmem] * 8,
        out_specs=(vmem, vmem, vmem) + (anywhere,) * 4,
        scratch_shapes=[
            pltpu.VMEM(hbm_f.shape, jnp.bfloat16),
            pltpu.VMEM(hbm_b.shape, jnp.float32),
            pltpu.VMEM(hbm_f.shape, jnp.bfloat16),
            pltpu.VMEM(hbm_b.shape, jnp.float32),
            pltpu.VMEM((slots, row_width), jnp.bfloat16),
            pltpu.VMEM((elements * nodes, row_width), jnp.bfloat16),
            pltpu.VMEM((elements, 3 * nodes, samples), jnp.float32),
            pltpu.VMEM((elements * nodes, row_width), jnp.bfloat16),
            pltpu.VMEM((elements * nodes, row_width), jnp.bfloat16),
            pltpu.VMEM((slots, row_width), jnp.float32),
            pltpu.VMEM(dam_field.shape, jnp.float32),
            pltpu.VMEM((slots, row_width), jnp.float32),
            pltpu.VMEM((groups, GROUP * nodes, slots), jnp.bfloat16),
            pltpu.VMEM((groups, GROUP * nodes, dam_field.shape[0]), jnp.bfloat16),
            pltpu.VMEM((groups, slots, GROUP * nodes), jnp.bfloat16),
            pltpu.VMEM((groups, dam_field.shape[0], GROUP * nodes), jnp.bfloat16),
            pltpu.VMEM(stiff_ref.shape, jnp.bfloat16),
            pltpu.VMEM((slots, row_count), jnp.bfloat16),
            pltpu.VMEM((dam_field.shape[0], 1), jnp.float32),
            pltpu.VMEM((row_count, 1), jnp.float32),
            pltpu.SemaphoreType.DMA((1 + 6 * ROUNDS,)),
        ],
        compiler_params=pltpu.CompilerParams(
            collective_id=0, has_side_effects=True, vmem_limit_bytes=60 * 1024 * 1024),
    )(stiff_coef, mass_coef, history, dam_field, conn_free, conn_dam, stiff_ref,
      dam_step.reshape(1, -1), reg_step.reshape(1, -1), pair_select)
    return (outs[0], outs[1], outs[2])


def solution(mesh):
    in_specs = (
        P(("reg", "dam"), None),
        P(("reg", "dam"), None),
        P(("reg", "dam"), None),
        P(("reg", "dam"), None),
        P(("reg", "dam"), None),
        P(),
        P(("reg", "dam")),
        P(("reg", "dam")),
        P(("reg", "dam")),
        P(("reg", "dam")),
    )
    out_specs = (P(("reg", "dam"), None), P(("reg", "dam"), None), P(("reg", "dam"), None))
    return jax.shard_map(shards, mesh=mesh, in_specs=in_specs, out_specs=out_specs, check_vma=False)
```

```python
import functools

import jax
import jax.numpy as jnp
from jax import lax
from jax.experimental import pallas as pl
from jax.experimental.pallas import tpu as pltpu
from jax.sharding import PartitionSpec as P

ROUNDS = 2
GROUP = 4
GATHER_PARTS = 4


def one_hot(indices, width):
    numbers = jnp.arange(width, dtype=jnp.int32)
    return (indices.reshape(-1)[:, None] == numbers[None, :]).astype(jnp.bfloat16)


def block_places(routes, devices, capacity):
    entries = routes.reshape(-1)
    numbers = jnp.arange(devices, dtype=jnp.int32)
    onehot = (entries[:, None] == numbers[None, :]).astype(jnp.int32)
    before = jnp.cumsum(onehot, axis=0) - onehot
    slot = jnp.sum(before * onehot, axis=1)
    return entries * capacity + slot


def coupling_kernel(n, ndam, sc_ref, mc_ref, hist_ref, dam_ref, cf_ref, cd_ref, stiff_ref,
                    dstep_row, rstep_row, q_ref,
                    hist_out, pulled_out, dam_out,
                    land_f0, land_f1, land_b0, land_b1,
                    stage_f, stage_b, landv_f, landv_b,
                    recv, ud_buf, ssd_buf, hi_buf, lo_buf, back, dsum, ret,
                    ohf_buf, ohd_buf, ohtf_buf, ohtd_buf, uf_buf, sp_ref, qt_ref, dstep_ref, rstep_ref,
                    sems):
    f32, bf16 = jnp.float32, jnp.bfloat16
    mesh_id = pl.DeviceIdType.MESH
    me = lax.axis_index("reg") * ndam + lax.axis_index("dam")
    slots = recv.shape[0]
    dcount = dam_out.shape[0]
    nodes = cf_ref.shape[1]
    width = GROUP * nodes
    groups = cf_ref.shape[0] // GROUP
    samples = recv.shape[1] // 3
    lands_f, lands_b = (land_f0, land_f1), (land_b0, land_b1)
    blocks = stage_f.shape

    barrier = pltpu.get_barrier_semaphore()

    def greet(step, carry):
        peer = lax.rem(me + step, n)
        pl.semaphore_signal(barrier, 1, device_id=(peer // ndam, peer % ndam),
                            device_id_type=mesh_id)
        return carry

    lax.fori_loop(1, n, greet, 0)

    def build_selectors(g, carry):
        for k in range(GROUP):
            lanes = slice(k * nodes, (k + 1) * nodes)
            cf = cf_ref[pl.ds(g * GROUP + k, 1), :]
            cd = cd_ref[pl.ds(g * GROUP + k, 1), :]
            ohtf_buf[g, :, lanes] = (
                lax.broadcasted_iota(jnp.int32, (slots, nodes), 0) == cf).astype(bf16)
            ohtd_buf[g, :, lanes] = (
                lax.broadcasted_iota(jnp.int32, (dcount, nodes), 0) == cd).astype(bf16)
        rows = pl.ds(pl.multiple_of(g * width, width), width)
        ohf_buf[rows, :] = jnp.transpose(ohtf_buf[g].astype(f32)).astype(bf16)
        ohd_buf[rows, :] = jnp.transpose(ohtd_buf[g].astype(f32)).astype(bf16)
        return carry

    lax.fori_loop(0, groups, build_selectors, 0)
    size = sp_ref.shape[0]
    across = lax.broadcasted_iota(jnp.int32, (size, size), 0)
    down = lax.broadcasted_iota(jnp.int32, (size, size), 1)
    pick_rows = (down == (across % nodes) * 3 + across // nodes).astype(bf16)
    pick_cols = (across == (down % nodes) * 3 + down // nodes).astype(bf16)
    permuted = jnp.dot(pick_rows, stiff_ref[...], preferred_element_type=f32).astype(bf16)
    sp_ref[...] = jnp.dot(permuted, pick_cols, preferred_element_type=f32).astype(bf16)
    qt_ref[...] = jnp.transpose(q_ref[...].astype(f32)).astype(bf16)
    dstep_ref[...] = jnp.transpose(
        jnp.broadcast_to(dstep_row[...], (8, dstep_row.shape[1])))[:, 0:1]
    rstep_ref[...] = jnp.transpose(
        jnp.broadcast_to(rstep_row[...], (8, rstep_row.shape[1])))[:, 0:1]
    pl.semaphore_wait(barrier, n - 1)

    def local_copy(src, dst):
        cp = pltpu.make_async_copy(src, dst, sems.at[0])
        cp.start()
        cp.wait()

    def start_exchange(stage, land, base):
        own = pltpu.make_async_copy(stage.at[me], land.at[me], sems.at[base + 2])
        own.start()

        def send(step, carry):
            peer = lax.rem(me + step, n)
            pltpu.make_async_remote_copy(
                src_ref=stage.at[peer],
                dst_ref=land.at[me],
                send_sem=sems.at[base],
                recv_sem=sems.at[base + 1],
                device_id=(peer // ndam, peer % ndam),
                device_id_type=mesh_id,
            ).start()
            return carry

        lax.fori_loop(1, n, send, 0)
        return own

    def finish_exchange(stage, land, base, own):
        everything = pltpu.make_async_remote_copy(
            src_ref=stage.at[pl.ds(0, n - 1)],
            dst_ref=land.at[pl.ds(0, n - 1)],
            send_sem=sems.at[base],
            recv_sem=sems.at[base + 1],
            device_id=(me // ndam, me % ndam),
            device_id_type=mesh_id,
        )
        everything.wait_send()
        everything.wait_recv()
        own.wait()

    def node_major(u, k):
        lo_row, hi_row = k * nodes, (k + 1) * nodes
        return jnp.concatenate(
            [u[lo_row:hi_row, c * samples:(c + 1) * samples] for c in range(3)], axis=0)

    def gather_all(select, table, out):
        for part in range(GATHER_PARTS):
            rows = slice(part * out.shape[0] // GATHER_PARTS, (part + 1) * out.shape[0] // GATHER_PARTS)
            out[rows, :] = jnp.dot(select[rows, :], table[...],
                                   preferred_element_type=f32).astype(bf16)

    def dam_side(g, carry):
        rows = pl.ds(pl.multiple_of(g * width, width), width)
        ud = ud_buf[rows, :]
        for k in range(GROUP):
            ssd_buf[g * GROUP + k] = jnp.dot(sp_ref[...], node_major(ud, k),
                                             preferred_element_type=f32)
        return carry

    def free_side(g, carry):
        rows = pl.ds(pl.multiple_of(g * width, width), width)
        uf = uf_buf[rows, :]
        ud = ud_buf[rows, :]
        forces = []
        for k in range(GROUP):
            e = g * GROUP + k
            wf = node_major(uf, k)
            wd = node_major(ud, k)
            ss = ssd_buf[e] + jnp.dot(sp_ref[...], wf, preferred_element_type=f32)
            tot = wf.astype(f32) + wd.astype(f32)
            lane = lax.broadcasted_iota(jnp.int32, tot.shape, 1)
            prev = jnp.where(lane == 0, 0.0, pltpu.roll(tot, 1, 1))
            nxt = jnp.where(lane == samples - 1, 0.0, pltpu.roll(tot, samples - 1, 1))
            accel = (nxt - 2.0 * tot) + prev
            f = sc_ref[e] * ss + mc_ref[e] * accel
            forces.append(
                jnp.concatenate([f[c * nodes:(c + 1) * nodes, :] for c in range(3)], axis=1))
        fg = jnp.concatenate(forces, axis=0)
        hi = fg.astype(bf16)
        lo = (fg - hi.astype(f32)).astype(bf16)
        hi_buf[rows, :] = hi
        lo_buf[rows, :] = lo
        both = jnp.dot(ohtf_buf[g], jnp.concatenate([hi, lo], axis=1),
                       preferred_element_type=f32)
        back[...] += both[:, :3 * samples] + both[:, 3 * samples:]
        return carry

    def dam_scatter(g, carry):
        rows = pl.ds(pl.multiple_of(g * width, width), width)
        both = jnp.dot(ohtd_buf[g], jnp.concatenate([hi_buf[rows, :], lo_buf[rows, :]], axis=1),
                       preferred_element_type=f32)
        dsum[...] += both[:, :3 * samples] + both[:, 3 * samples:]
        return carry

    hist_out[...] = hist_ref[...]
    dam_out[...] = dam_ref[...]
    for r in range(ROUNDS):
        base_f, base_b = 1 + 6 * r, 4 + 6 * r
        outgoing = jnp.dot(qt_ref[...], hist_out[...], preferred_element_type=f32).astype(bf16)
        stage_f[...] = outgoing.reshape(blocks)
        own_f = start_exchange(stage_f, lands_f[r], base_f)
        gather_all(ohd_buf, dam_out, ud_buf)
        lax.fori_loop(0, groups, dam_side, 0)
        finish_exchange(stage_f, lands_f[r], base_f, own_f)
        local_copy(lands_f[r], landv_f)
        recv[...] = landv_f[...].reshape(recv.shape)

        back[...] = jnp.zeros(back.shape, f32)
        gather_all(ohf_buf, recv, uf_buf)
        lax.fori_loop(0, groups, free_side, 0)
        stage_b[...] = back[...].reshape(blocks)
        own_b = start_exchange(stage_b, lands_b[r], base_b)
        dsum[...] = jnp.zeros(dsum.shape, f32)
        lax.fori_loop(0, groups, dam_scatter, 0)
        dam_out[...] = (dam_out[...].astype(f32) - dstep_ref[...] * dsum[...]).astype(bf16)
        finish_exchange(stage_b, lands_b[r], base_b, own_b)
        local_copy(lands_b[r], landv_b)
        ret[...] = landv_b[...].reshape(ret.shape)

        returned = ret[...]
        ret_hi = returned.astype(bf16)
        ret_lo = (returned - ret_hi.astype(f32)).astype(bf16)
        pulled = (jnp.dot(q_ref[...], ret_hi, preferred_element_type=f32)
                  + jnp.dot(q_ref[...], ret_lo, preferred_element_type=f32))
        hist_out[...] = (hist_out[...].astype(f32) - rstep_ref[...] * pulled).astype(bf16)
        if r == ROUNDS - 1:
            pulled_out[...] = pulled


def shards(history, routes, dam_field, conn_free, conn_dam, stiff_ref, stiff_coef,
           mass_coef, reg_step, dam_step):
    devices = lax.axis_size(("reg", "dam"))
    ndam = lax.axis_size("dam")
    row_count, row_width = history.shape
    capacity = 4 * row_count // devices
    slots = devices * capacity
    nodes = conn_free.shape[1]
    samples = row_width // 3
    places = block_places(routes, devices, capacity)
    pair_select = one_hot(places, slots).reshape(row_count, 2, slots).sum(axis=1)
    smem = pl.BlockSpec(memory_space=pltpu.SMEM)
    vmem = pl.BlockSpec(memory_space=pltpu.VMEM)
    anywhere = pl.BlockSpec(memory_space=pl.ANY)
    elements = conn_free.shape[0]
    groups = conn_free.shape[0] // GROUP
    hbm_f = jax.ShapeDtypeStruct((devices, capacity, row_width), jnp.bfloat16)
    hbm_b = jax.ShapeDtypeStruct((devices, capacity, row_width), jnp.float32)
    outs = pl.pallas_call(
        functools.partial(coupling_kernel, devices, ndam),
        out_shape=(
            jax.ShapeDtypeStruct(history.shape, jnp.bfloat16),
            jax.ShapeDtypeStruct(history.shape, jnp.float32),
            jax.ShapeDtypeStruct(dam_field.shape, jnp.bfloat16),
            hbm_f, hbm_f, hbm_b, hbm_b,
        ),
        in_specs=[smem, smem] + [vmem] * 8,
        out_specs=(vmem, vmem, vmem) + (anywhere,) * 4,
        scratch_shapes=[
            pltpu.VMEM(hbm_f.shape, jnp.bfloat16),
            pltpu.VMEM(hbm_b.shape, jnp.float32),
            pltpu.VMEM(hbm_f.shape, jnp.bfloat16),
            pltpu.VMEM(hbm_b.shape, jnp.float32),
            pltpu.VMEM((slots, row_width), jnp.bfloat16),
            pltpu.VMEM((elements * nodes, row_width), jnp.bfloat16),
            pltpu.VMEM((elements, 3 * nodes, samples), jnp.float32),
            pltpu.VMEM((elements * nodes, row_width), jnp.bfloat16),
            pltpu.VMEM((elements * nodes, row_width), jnp.bfloat16),
            pltpu.VMEM((slots, row_width), jnp.float32),
            pltpu.VMEM(dam_field.shape, jnp.float32),
            pltpu.VMEM((slots, row_width), jnp.float32),
            pltpu.VMEM((elements * nodes, slots), jnp.bfloat16),
            pltpu.VMEM((elements * nodes, dam_field.shape[0]), jnp.bfloat16),
            pltpu.VMEM((groups, slots, GROUP * nodes), jnp.bfloat16),
            pltpu.VMEM((groups, dam_field.shape[0], GROUP * nodes), jnp.bfloat16),
            pltpu.VMEM((elements * nodes, row_width), jnp.bfloat16),
            pltpu.VMEM(stiff_ref.shape, jnp.bfloat16),
            pltpu.VMEM((slots, row_count), jnp.bfloat16),
            pltpu.VMEM((dam_field.shape[0], 1), jnp.float32),
            pltpu.VMEM((row_count, 1), jnp.float32),
            pltpu.SemaphoreType.DMA((1 + 6 * ROUNDS,)),
        ],
        compiler_params=pltpu.CompilerParams(
            collective_id=0, has_side_effects=True, vmem_limit_bytes=60 * 1024 * 1024),
    )(stiff_coef, mass_coef, history, dam_field, conn_free, conn_dam, stiff_ref,
      dam_step.reshape(1, -1), reg_step.reshape(1, -1), pair_select)
    return (outs[0], outs[1], outs[2])


def solution(mesh):
    in_specs = (
        P(("reg", "dam"), None),
        P(("reg", "dam"), None),
        P(("reg", "dam"), None),
        P(("reg", "dam"), None),
        P(("reg", "dam"), None),
        P(),
        P(("reg", "dam")),
        P(("reg", "dam")),
        P(("reg", "dam")),
        P(("reg", "dam")),
    )
    out_specs = (P(("reg", "dam"), None), P(("reg", "dam"), None), P(("reg", "dam"), None))
    return jax.shard_map(shards, mesh=mesh, in_specs=in_specs, out_specs=out_specs, check_vma=False)
```

```python
import functools

import jax
import jax.numpy as jnp
from jax import lax
from jax.experimental import pallas as pl
from jax.experimental.pallas import tpu as pltpu
from jax.sharding import PartitionSpec as P

ROUNDS = 2
GROUP = 4
GATHER_PARTS = 4


def one_hot(indices, width):
    numbers = jnp.arange(width, dtype=jnp.int32)
    return (indices.reshape(-1)[:, None] == numbers[None, :]).astype(jnp.bfloat16)


def block_places(routes, devices, capacity):
    entries = routes.reshape(-1)
    numbers = jnp.arange(devices, dtype=jnp.int32)
    onehot = (entries[:, None] == numbers[None, :]).astype(jnp.int32)
    before = jnp.cumsum(onehot, axis=0) - onehot
    slot = jnp.sum(before * onehot, axis=1)
    return entries * capacity + slot


def coupling_kernel(n, ndam, sc_ref, mc_ref, hist_ref, dam_ref, cf_ref, cd_ref, stiff_ref,
                    dstep_row, rstep_row, q_ref,
                    hist_out, pulled_out, dam_out,
                    land_f0, land_f1, land_b0, land_b1,
                    stage_f, stage_b, landv_f, landv_b,
                    recv, ud_buf, ssd_buf, hi_buf, lo_buf, back, dsum, ret,
                    ohf_buf, ohd_buf, ohtf_buf, ohtd_buf, uf_buf, sp_ref, qt_ref, dstep_ref, rstep_ref,
                    sems):
    f32, bf16 = jnp.float32, jnp.bfloat16
    mesh_id = pl.DeviceIdType.MESH
    me = lax.axis_index("reg") * ndam + lax.axis_index("dam")
    slots = recv.shape[0]
    dcount = dam_out.shape[0]
    nodes = cf_ref.shape[1]
    width = GROUP * nodes
    groups = cf_ref.shape[0] // GROUP
    samples = recv.shape[1] // 3
    lands_f, lands_b = (land_f0, land_f1), (land_b0, land_b1)
    blocks = stage_f.shape

    barrier = pltpu.get_barrier_semaphore()

    def greet(step, carry):
        peer = lax.rem(me + step, n)
        pl.semaphore_signal(barrier, 1, device_id=(peer // ndam, peer % ndam),
                            device_id_type=mesh_id)
        return carry

    lax.fori_loop(1, n, greet, 0)

    def build_selectors(g, carry):
        for k in range(GROUP):
            lanes = slice(k * nodes, (k + 1) * nodes)
            cf = cf_ref[pl.ds(g * GROUP + k, 1), :]
            cd = cd_ref[pl.ds(g * GROUP + k, 1), :]
            ohtf_buf[g, :, lanes] = (
                lax.broadcasted_iota(jnp.int32, (slots, nodes), 0) == cf).astype(bf16)
            ohtd_buf[g, :, lanes] = (
                lax.broadcasted_iota(jnp.int32, (dcount, nodes), 0) == cd).astype(bf16)
        rows = pl.ds(pl.multiple_of(g * width, width), width)
        ohf_buf[rows, :] = jnp.transpose(ohtf_buf[g].astype(f32)).astype(bf16)
        ohd_buf[rows, :] = jnp.transpose(ohtd_buf[g].astype(f32)).astype(bf16)
        return carry

    lax.fori_loop(0, groups, build_selectors, 0)
    size = sp_ref.shape[0]
    across = lax.broadcasted_iota(jnp.int32, (size, size), 0)
    down = lax.broadcasted_iota(jnp.int32, (size, size), 1)
    pick_rows = (down == (across % nodes) * 3 + across // nodes).astype(bf16)
    pick_cols = (across == (down % nodes) * 3 + down // nodes).astype(bf16)
    permuted = jnp.dot(pick_rows, stiff_ref[...], preferred_element_type=f32).astype(bf16)
    sp_ref[...] = jnp.dot(permuted, pick_cols, preferred_element_type=f32).astype(bf16)
    qt_ref[...] = jnp.transpose(q_ref[...].astype(f32)).astype(bf16)
    dstep_ref[...] = jnp.transpose(
        jnp.broadcast_to(dstep_row[...], (8, dstep_row.shape[1])))[:, 0:1]
    rstep_ref[...] = jnp.transpose(
        jnp.broadcast_to(rstep_row[...], (8, rstep_row.shape[1])))[:, 0:1]
    pl.semaphore_wait(barrier, n - 1)

    def local_copy(src, dst):
        cp = pltpu.make_async_copy(src, dst, sems.at[0])
        cp.start()
        cp.wait()

    def start_exchange(stage, land, base):
        own = pltpu.make_async_copy(stage.at[me], land.at[me], sems.at[base + 2])
        own.start()

        def send(step, carry):
            peer = lax.rem(me + step, n)
            pltpu.make_async_remote_copy(
                src_ref=stage.at[peer],
                dst_ref=land.at[me],
                send_sem=sems.at[base],
                recv_sem=sems.at[base + 1],
                device_id=(peer // ndam, peer % ndam),
                device_id_type=mesh_id,
            ).start()
            return carry

        lax.fori_loop(1, n, send, 0)
        return own

    def finish_exchange(stage, land, base, own):
        everything = pltpu.make_async_remote_copy(
            src_ref=stage.at[pl.ds(0, n - 1)],
            dst_ref=land.at[pl.ds(0, n - 1)],
            send_sem=sems.at[base],
            recv_sem=sems.at[base + 1],
            device_id=(me // ndam, me % ndam),
            device_id_type=mesh_id,
        )
        everything.wait_send()
        everything.wait_recv()
        own.wait()

    def node_major(u, k):
        lo_row, hi_row = k * nodes, (k + 1) * nodes
        return jnp.concatenate(
            [u[lo_row:hi_row, c * samples:(c + 1) * samples] for c in range(3)], axis=0)

    def gather_all(select, table, out):
        for part in range(GATHER_PARTS):
            rows = slice(part * out.shape[0] // GATHER_PARTS, (part + 1) * out.shape[0] // GATHER_PARTS)
            out[rows, :] = jnp.dot(select[rows, :], table[...],
                                   preferred_element_type=f32).astype(bf16)

    def dam_side(g, carry):
        rows = pl.ds(pl.multiple_of(g * width, width), width)
        ud = ud_buf[rows, :]
        side = jnp.concatenate([node_major(ud, k) for k in range(GROUP)], axis=1)
        ssd_buf[g] = jnp.dot(sp_ref[...], side, preferred_element_type=f32)
        return carry

    def free_side(g, carry):
        rows = pl.ds(pl.multiple_of(g * width, width), width)
        uf = uf_buf[rows, :]
        ud = ud_buf[rows, :]
        forces = []
        free_all = [node_major(uf, k) for k in range(GROUP)]
        ss_all = ssd_buf[g] + jnp.dot(sp_ref[...], jnp.concatenate(free_all, axis=1),
                                      preferred_element_type=f32)
        for k in range(GROUP):
            e = g * GROUP + k
            wf = free_all[k]
            wd = node_major(ud, k)
            ss = ss_all[:, k * samples:(k + 1) * samples]
            tot = wf.astype(f32) + wd.astype(f32)
            lane = lax.broadcasted_iota(jnp.int32, tot.shape, 1)
            prev = jnp.where(lane == 0, 0.0, pltpu.roll(tot, 1, 1))
            nxt = jnp.where(lane == samples - 1, 0.0, pltpu.roll(tot, samples - 1, 1))
            accel = (nxt - 2.0 * tot) + prev
            f = sc_ref[e] * ss + mc_ref[e] * accel
            forces.append(
                jnp.concatenate([f[c * nodes:(c + 1) * nodes, :] for c in range(3)], axis=1))
        fg = jnp.concatenate(forces, axis=0)
        hi = fg.astype(bf16)
        lo = (fg - hi.astype(f32)).astype(bf16)
        hi_buf[rows, :] = hi
        lo_buf[rows, :] = lo
        both = jnp.dot(ohtf_buf[g], jnp.concatenate([hi, lo], axis=1),
                       preferred_element_type=f32)
        back[...] += both[:, :3 * samples] + both[:, 3 * samples:]
        return carry

    def dam_scatter(g, carry):
        rows = pl.ds(pl.multiple_of(g * width, width), width)
        both = jnp.dot(ohtd_buf[g], jnp.concatenate([hi_buf[rows, :], lo_buf[rows, :]], axis=1),
                       preferred_element_type=f32)
        dsum[...] += both[:, :3 * samples] + both[:, 3 * samples:]
        return carry

    hist_out[...] = hist_ref[...]
    dam_out[...] = dam_ref[...]
    for r in range(ROUNDS):
        base_f, base_b = 1 + 6 * r, 4 + 6 * r
        outgoing = jnp.dot(qt_ref[...], hist_out[...], preferred_element_type=f32).astype(bf16)
        stage_f[...] = outgoing.reshape(blocks)
        own_f = start_exchange(stage_f, lands_f[r], base_f)
        gather_all(ohd_buf, dam_out, ud_buf)
        lax.fori_loop(0, groups, dam_side, 0)
        finish_exchange(stage_f, lands_f[r], base_f, own_f)
        local_copy(lands_f[r], landv_f)
        recv[...] = landv_f[...].reshape(recv.shape)

        back[...] = jnp.zeros(back.shape, f32)
        gather_all(ohf_buf, recv, uf_buf)
        lax.fori_loop(0, groups, free_side, 0)
        stage_b[...] = back[...].reshape(blocks)
        own_b = start_exchange(stage_b, lands_b[r], base_b)
        dsum[...] = jnp.zeros(dsum.shape, f32)
        lax.fori_loop(0, groups, dam_scatter, 0)
        dam_out[...] = (dam_out[...].astype(f32) - dstep_ref[...] * dsum[...]).astype(bf16)
        finish_exchange(stage_b, lands_b[r], base_b, own_b)
        local_copy(lands_b[r], landv_b)
        ret[...] = landv_b[...].reshape(ret.shape)

        returned = ret[...]
        ret_hi = returned.astype(bf16)
        ret_lo = (returned - ret_hi.astype(f32)).astype(bf16)
        pulled = (jnp.dot(q_ref[...], ret_hi, preferred_element_type=f32)
                  + jnp.dot(q_ref[...], ret_lo, preferred_element_type=f32))
        hist_out[...] = (hist_out[...].astype(f32) - rstep_ref[...] * pulled).astype(bf16)
        if r == ROUNDS - 1:
            pulled_out[...] = pulled


def shards(history, routes, dam_field, conn_free, conn_dam, stiff_ref, stiff_coef,
           mass_coef, reg_step, dam_step):
    devices = lax.axis_size(("reg", "dam"))
    ndam = lax.axis_size("dam")
    row_count, row_width = history.shape
    capacity = 4 * row_count // devices
    slots = devices * capacity
    nodes = conn_free.shape[1]
    samples = row_width // 3
    places = block_places(routes, devices, capacity)
    pair_select = one_hot(places, slots).reshape(row_count, 2, slots).sum(axis=1)
    smem = pl.BlockSpec(memory_space=pltpu.SMEM)
    vmem = pl.BlockSpec(memory_space=pltpu.VMEM)
    anywhere = pl.BlockSpec(memory_space=pl.ANY)
    elements = conn_free.shape[0]
    groups = conn_free.shape[0] // GROUP
    hbm_f = jax.ShapeDtypeStruct((devices, capacity, row_width), jnp.bfloat16)
    hbm_b = jax.ShapeDtypeStruct((devices, capacity, row_width), jnp.float32)
    outs = pl.pallas_call(
        functools.partial(coupling_kernel, devices, ndam),
        out_shape=(
            jax.ShapeDtypeStruct(history.shape, jnp.bfloat16),
            jax.ShapeDtypeStruct(history.shape, jnp.float32),
            jax.ShapeDtypeStruct(dam_field.shape, jnp.bfloat16),
            hbm_f, hbm_f, hbm_b, hbm_b,
        ),
        in_specs=[smem, smem] + [vmem] * 8,
        out_specs=(vmem, vmem, vmem) + (anywhere,) * 4,
        scratch_shapes=[
            pltpu.VMEM(hbm_f.shape, jnp.bfloat16),
            pltpu.VMEM(hbm_b.shape, jnp.float32),
            pltpu.VMEM(hbm_f.shape, jnp.bfloat16),
            pltpu.VMEM(hbm_b.shape, jnp.float32),
            pltpu.VMEM((slots, row_width), jnp.bfloat16),
            pltpu.VMEM((elements * nodes, row_width), jnp.bfloat16),
            pltpu.VMEM((groups, 3 * nodes, GROUP * samples), jnp.float32),
            pltpu.VMEM((elements * nodes, row_width), jnp.bfloat16),
            pltpu.VMEM((elements * nodes, row_width), jnp.bfloat16),
            pltpu.VMEM((slots, row_width), jnp.float32),
            pltpu.VMEM(dam_field.shape, jnp.float32),
            pltpu.VMEM((slots, row_width), jnp.float32),
            pltpu.VMEM((elements * nodes, slots), jnp.bfloat16),
            pltpu.VMEM((elements * nodes, dam_field.shape[0]), jnp.bfloat16),
            pltpu.VMEM((groups, slots, GROUP * nodes), jnp.bfloat16),
            pltpu.VMEM((groups, dam_field.shape[0], GROUP * nodes), jnp.bfloat16),
            pltpu.VMEM((elements * nodes, row_width), jnp.bfloat16),
            pltpu.VMEM(stiff_ref.shape, jnp.bfloat16),
            pltpu.VMEM((slots, row_count), jnp.bfloat16),
            pltpu.VMEM((dam_field.shape[0], 1), jnp.float32),
            pltpu.VMEM((row_count, 1), jnp.float32),
            pltpu.SemaphoreType.DMA((1 + 6 * ROUNDS,)),
        ],
        compiler_params=pltpu.CompilerParams(
            collective_id=0, has_side_effects=True, vmem_limit_bytes=60 * 1024 * 1024),
    )(stiff_coef, mass_coef, history, dam_field, conn_free, conn_dam, stiff_ref,
      dam_step.reshape(1, -1), reg_step.reshape(1, -1), pair_select)
    return (outs[0], outs[1], outs[2])


def solution(mesh):
    in_specs = (
        P(("reg", "dam"), None),
        P(("reg", "dam"), None),
        P(("reg", "dam"), None),
        P(("reg", "dam"), None),
        P(("reg", "dam"), None),
        P(),
        P(("reg", "dam")),
        P(("reg", "dam")),
        P(("reg", "dam")),
        P(("reg", "dam")),
    )
    out_specs = (P(("reg", "dam"), None), P(("reg", "dam"), None), P(("reg", "dam"), None))
    return jax.shard_map(shards, mesh=mesh, in_specs=in_specs, out_specs=out_specs, check_vma=False)
```

```python
import functools

import jax
import jax.numpy as jnp
from jax import lax
from jax.experimental import pallas as pl
from jax.experimental.pallas import tpu as pltpu
from jax.sharding import PartitionSpec as P

ROUNDS = 2
GROUP = 4
GATHER_PARTS = 4


def coupling_kernel(n, ndam, sc_ref, mc_ref, hist_ref, dam_ref, cf_ref, cd_ref, stiff_ref,
                    dstep_row, rstep_row, routes_ref,
                    hist_out, pulled_out, dam_out,
                    land_f0, land_f1, land_b0, land_b1,
                    stage_f, stage_b, landv_f, landv_b,
                    recv, ud_buf, ssd_buf, hi_buf, lo_buf, back, dsum, ret,
                    ohf_buf, ohd_buf, ohtf_buf, ohtd_buf, uf_buf, sp_ref, q_ref, qt_ref, dstep_ref, rstep_ref,
                    sems):
    f32, bf16 = jnp.float32, jnp.bfloat16
    mesh_id = pl.DeviceIdType.MESH
    me = lax.axis_index("reg") * ndam + lax.axis_index("dam")
    slots = recv.shape[0]
    dcount = dam_out.shape[0]
    nodes = cf_ref.shape[1]
    width = GROUP * nodes
    groups = cf_ref.shape[0] // GROUP
    samples = recv.shape[1] // 3
    lands_f, lands_b = (land_f0, land_f1), (land_b0, land_b1)
    blocks = stage_f.shape

    barrier = pltpu.get_barrier_semaphore()

    def greet(step, carry):
        peer = lax.rem(me + step, n)
        pl.semaphore_signal(barrier, 1, device_id=(peer // ndam, peer % ndam),
                            device_id_type=mesh_id)
        return carry

    lax.fori_loop(1, n, greet, 0)

    def build_selectors(g, carry):
        for k in range(GROUP):
            lanes = slice(k * nodes, (k + 1) * nodes)
            cf = cf_ref[pl.ds(g * GROUP + k, 1), :]
            cd = cd_ref[pl.ds(g * GROUP + k, 1), :]
            ohtf_buf[g, :, lanes] = (
                lax.broadcasted_iota(jnp.int32, (slots, nodes), 0) == cf).astype(bf16)
            ohtd_buf[g, :, lanes] = (
                lax.broadcasted_iota(jnp.int32, (dcount, nodes), 0) == cd).astype(bf16)
        rows = pl.ds(pl.multiple_of(g * width, width), width)
        ohf_buf[rows, :] = jnp.transpose(ohtf_buf[g].astype(f32)).astype(bf16)
        ohd_buf[rows, :] = jnp.transpose(ohtd_buf[g].astype(f32)).astype(bf16)
        return carry

    lax.fori_loop(0, groups, build_selectors, 0)
    size = sp_ref.shape[0]
    across = lax.broadcasted_iota(jnp.int32, (size, size), 0)
    down = lax.broadcasted_iota(jnp.int32, (size, size), 1)
    pick_rows = (down == (across % nodes) * 3 + across // nodes).astype(bf16)
    pick_cols = (across == (down % nodes) * 3 + down // nodes).astype(bf16)
    permuted = jnp.dot(pick_rows, stiff_ref[...], preferred_element_type=f32).astype(bf16)
    sp_ref[...] = jnp.dot(permuted, pick_cols, preferred_element_type=f32).astype(bf16)
    regional = routes_ref.shape[0]
    capacity = slots // n
    first = routes_ref[:, 0:1]
    second = routes_ref[:, 1:2]
    numbers = lax.broadcasted_iota(jnp.int32, (regional, n), 1)
    hit_first = (first == numbers).astype(f32)
    hit_second = (second == numbers).astype(f32)
    earlier = (lax.broadcasted_iota(jnp.int32, (regional, regional), 1)
               < lax.broadcasted_iota(jnp.int32, (regional, regional), 0)).astype(bf16)
    counts = jnp.dot(earlier, (hit_first + hit_second).astype(bf16), preferred_element_type=f32)
    slot_first = jnp.sum(counts * hit_first, axis=1, keepdims=True).astype(jnp.int32)
    slot_second = jnp.sum(counts * hit_second, axis=1, keepdims=True).astype(jnp.int32)
    place_first = first * capacity + slot_first
    place_second = second * capacity + slot_second
    columns = lax.broadcasted_iota(jnp.int32, (regional, slots), 1)
    pair = jnp.logical_or(columns == place_first, columns == place_second).astype(f32)
    q_ref[...] = pair.astype(bf16)
    qt_ref[...] = jnp.transpose(pair).astype(bf16)
    dstep_ref[...] = jnp.transpose(
        jnp.broadcast_to(dstep_row[...], (8, dstep_row.shape[1])))[:, 0:1]
    rstep_ref[...] = jnp.transpose(
        jnp.broadcast_to(rstep_row[...], (8, rstep_row.shape[1])))[:, 0:1]
    pl.semaphore_wait(barrier, n - 1)

    def local_copy(src, dst):
        cp = pltpu.make_async_copy(src, dst, sems.at[0])
        cp.start()
        cp.wait()

    def start_exchange(stage, land, base):
        own = pltpu.make_async_copy(stage.at[me], land.at[me], sems.at[base + 2])
        own.start()

        def send(step, carry):
            peer = lax.rem(me + step, n)
            pltpu.make_async_remote_copy(
                src_ref=stage.at[peer],
                dst_ref=land.at[me],
                send_sem=sems.at[base],
                recv_sem=sems.at[base + 1],
                device_id=(peer // ndam, peer % ndam),
                device_id_type=mesh_id,
            ).start()
            return carry

        lax.fori_loop(1, n, send, 0)
        return own

    def finish_exchange(stage, land, base, own):
        everything = pltpu.make_async_remote_copy(
            src_ref=stage.at[pl.ds(0, n - 1)],
            dst_ref=land.at[pl.ds(0, n - 1)],
            send_sem=sems.at[base],
            recv_sem=sems.at[base + 1],
            device_id=(me // ndam, me % ndam),
            device_id_type=mesh_id,
        )
        everything.wait_send()
        everything.wait_recv()
        own.wait()

    def node_major(u, k):
        lo_row, hi_row = k * nodes, (k + 1) * nodes
        return jnp.concatenate(
            [u[lo_row:hi_row, c * samples:(c + 1) * samples] for c in range(3)], axis=0)

    def gather_all(select, table, out):
        for part in range(GATHER_PARTS):
            rows = slice(part * out.shape[0] // GATHER_PARTS, (part + 1) * out.shape[0] // GATHER_PARTS)
            out[rows, :] = jnp.dot(select[rows, :], table[...],
                                   preferred_element_type=f32).astype(bf16)

    def dam_side(g, carry):
        rows = pl.ds(pl.multiple_of(g * width, width), width)
        ud = ud_buf[rows, :]
        side = jnp.concatenate([node_major(ud, k) for k in range(GROUP)], axis=1)
        ssd_buf[g] = jnp.dot(sp_ref[...], side, preferred_element_type=f32)
        return carry

    def free_side(g, carry):
        rows = pl.ds(pl.multiple_of(g * width, width), width)
        uf = uf_buf[rows, :]
        ud = ud_buf[rows, :]
        forces = []
        free_all = [node_major(uf, k) for k in range(GROUP)]
        ss_all = ssd_buf[g] + jnp.dot(sp_ref[...], jnp.concatenate(free_all, axis=1),
                                      preferred_element_type=f32)
        for k in range(GROUP):
            e = g * GROUP + k
            wf = free_all[k]
            wd = node_major(ud, k)
            ss = ss_all[:, k * samples:(k + 1) * samples]
            tot = wf.astype(f32) + wd.astype(f32)
            lane = lax.broadcasted_iota(jnp.int32, tot.shape, 1)
            prev = jnp.where(lane == 0, 0.0, pltpu.roll(tot, 1, 1))
            nxt = jnp.where(lane == samples - 1, 0.0, pltpu.roll(tot, samples - 1, 1))
            accel = (nxt - 2.0 * tot) + prev
            f = sc_ref[e] * ss + mc_ref[e] * accel
            forces.append(
                jnp.concatenate([f[c * nodes:(c + 1) * nodes, :] for c in range(3)], axis=1))
        fg = jnp.concatenate(forces, axis=0)
        hi = fg.astype(bf16)
        lo = (fg - hi.astype(f32)).astype(bf16)
        hi_buf[rows, :] = hi
        lo_buf[rows, :] = lo
        both = jnp.dot(ohtf_buf[g], jnp.concatenate([hi, lo], axis=1),
                       preferred_element_type=f32)
        back[...] += both[:, :3 * samples] + both[:, 3 * samples:]
        return carry

    def dam_scatter(g, carry):
        rows = pl.ds(pl.multiple_of(g * width, width), width)
        both = jnp.dot(ohtd_buf[g], jnp.concatenate([hi_buf[rows, :], lo_buf[rows, :]], axis=1),
                       preferred_element_type=f32)
        dsum[...] += both[:, :3 * samples] + both[:, 3 * samples:]
        return carry

    hist_out[...] = hist_ref[...]
    dam_out[...] = dam_ref[...]
    for r in range(ROUNDS):
        base_f, base_b = 1 + 6 * r, 4 + 6 * r
        outgoing = jnp.dot(qt_ref[...], hist_out[...], preferred_element_type=f32).astype(bf16)
        stage_f[...] = outgoing.reshape(blocks)
        own_f = start_exchange(stage_f, lands_f[r], base_f)
        gather_all(ohd_buf, dam_out, ud_buf)
        lax.fori_loop(0, groups, dam_side, 0)
        finish_exchange(stage_f, lands_f[r], base_f, own_f)
        local_copy(lands_f[r], landv_f)
        recv[...] = landv_f[...].reshape(recv.shape)

        back[...] = jnp.zeros(back.shape, f32)
        gather_all(ohf_buf, recv, uf_buf)
        lax.fori_loop(0, groups, free_side, 0)
        stage_b[...] = back[...].reshape(blocks)
        own_b = start_exchange(stage_b, lands_b[r], base_b)
        dsum[...] = jnp.zeros(dsum.shape, f32)
        lax.fori_loop(0, groups, dam_scatter, 0)
        dam_out[...] = (dam_out[...].astype(f32) - dstep_ref[...] * dsum[...]).astype(bf16)
        finish_exchange(stage_b, lands_b[r], base_b, own_b)
        local_copy(lands_b[r], landv_b)
        ret[...] = landv_b[...].reshape(ret.shape)

        returned = ret[...]
        ret_hi = returned.astype(bf16)
        ret_lo = (returned - ret_hi.astype(f32)).astype(bf16)
        pulled = (jnp.dot(q_ref[...], ret_hi, preferred_element_type=f32)
                  + jnp.dot(q_ref[...], ret_lo, preferred_element_type=f32))
        hist_out[...] = (hist_out[...].astype(f32) - rstep_ref[...] * pulled).astype(bf16)
        if r == ROUNDS - 1:
            pulled_out[...] = pulled


def shards(history, routes, dam_field, conn_free, conn_dam, stiff_ref, stiff_coef,
           mass_coef, reg_step, dam_step):
    devices = lax.axis_size(("reg", "dam"))
    ndam = lax.axis_size("dam")
    row_count, row_width = history.shape
    capacity = 4 * row_count // devices
    slots = devices * capacity
    nodes = conn_free.shape[1]
    samples = row_width // 3
    smem = pl.BlockSpec(memory_space=pltpu.SMEM)
    vmem = pl.BlockSpec(memory_space=pltpu.VMEM)
    anywhere = pl.BlockSpec(memory_space=pl.ANY)
    elements = conn_free.shape[0]
    groups = conn_free.shape[0] // GROUP
    hbm_f = jax.ShapeDtypeStruct((devices, capacity, row_width), jnp.bfloat16)
    hbm_b = jax.ShapeDtypeStruct((devices, capacity, row_width), jnp.float32)
    outs = pl.pallas_call(
        functools.partial(coupling_kernel, devices, ndam),
        out_shape=(
            jax.ShapeDtypeStruct(history.shape, jnp.bfloat16),
            jax.ShapeDtypeStruct(history.shape, jnp.float32),
            jax.ShapeDtypeStruct(dam_field.shape, jnp.bfloat16),
            hbm_f, hbm_f, hbm_b, hbm_b,
        ),
        in_specs=[smem, smem] + [vmem] * 8,
        out_specs=(vmem, vmem, vmem) + (anywhere,) * 4,
        scratch_shapes=[
            pltpu.VMEM(hbm_f.shape, jnp.bfloat16),
            pltpu.VMEM(hbm_b.shape, jnp.float32),
            pltpu.VMEM(hbm_f.shape, jnp.bfloat16),
            pltpu.VMEM(hbm_b.shape, jnp.float32),
            pltpu.VMEM((slots, row_width), jnp.bfloat16),
            pltpu.VMEM((elements * nodes, row_width), jnp.bfloat16),
            pltpu.VMEM((groups, 3 * nodes, GROUP * samples), jnp.float32),
            pltpu.VMEM((elements * nodes, row_width), jnp.bfloat16),
            pltpu.VMEM((elements * nodes, row_width), jnp.bfloat16),
            pltpu.VMEM((slots, row_width), jnp.float32),
            pltpu.VMEM(dam_field.shape, jnp.float32),
            pltpu.VMEM((slots, row_width), jnp.float32),
            pltpu.VMEM((elements * nodes, slots), jnp.bfloat16),
            pltpu.VMEM((elements * nodes, dam_field.shape[0]), jnp.bfloat16),
            pltpu.VMEM((groups, slots, GROUP * nodes), jnp.bfloat16),
            pltpu.VMEM((groups, dam_field.shape[0], GROUP * nodes), jnp.bfloat16),
            pltpu.VMEM((elements * nodes, row_width), jnp.bfloat16),
            pltpu.VMEM(stiff_ref.shape, jnp.bfloat16),
            pltpu.VMEM((row_count, slots), jnp.bfloat16),
            pltpu.VMEM((slots, row_count), jnp.bfloat16),
            pltpu.VMEM((dam_field.shape[0], 1), jnp.float32),
            pltpu.VMEM((row_count, 1), jnp.float32),
            pltpu.SemaphoreType.DMA((1 + 6 * ROUNDS,)),
        ],
        compiler_params=pltpu.CompilerParams(
            collective_id=0, has_side_effects=True, vmem_limit_bytes=60 * 1024 * 1024),
    )(stiff_coef, mass_coef, history, dam_field, conn_free, conn_dam, stiff_ref,
      dam_step.reshape(1, -1), reg_step.reshape(1, -1), routes)
    return (outs[0], outs[1], outs[2])


def solution(mesh):
    in_specs = (
        P(("reg", "dam"), None),
        P(("reg", "dam"), None),
        P(("reg", "dam"), None),
        P(("reg", "dam"), None),
        P(("reg", "dam"), None),
        P(),
        P(("reg", "dam")),
        P(("reg", "dam")),
        P(("reg", "dam")),
        P(("reg", "dam")),
    )
    out_specs = (P(("reg", "dam"), None), P(("reg", "dam"), None), P(("reg", "dam"), None))
    return jax.shard_map(shards, mesh=mesh, in_specs=in_specs, out_specs=out_specs, check_vma=False)
```

```python
import functools

import jax
import jax.numpy as jnp
from jax import lax
from jax.experimental import pallas as pl
from jax.experimental.pallas import tpu as pltpu
from jax.sharding import PartitionSpec as P

ROUNDS = 2
GROUP = 4
GATHER_PARTS = 4


def coupling_kernel(n, ndam, sc_ref, mc_ref, hist_ref, dam_ref, cf_ref, cd_ref, stiff_ref,
                    dstep_row, rstep_row, routes_ref,
                    hist_out, pulled_out, dam_out,
                    land_f0, land_f1, land_b0, land_b1,
                    stage_f, stage_b, landv_f, landv_b,
                    recv, ud_buf, ssd_buf, hi_buf, lo_buf, back, dsum, ret,
                    ohf_buf, ohd_buf, ohtf_buf, ohtd_buf, uf_buf, sp_ref, q_ref, qt_ref, dstep_ref, rstep_ref,
                    sems):
    f32, bf16 = jnp.float32, jnp.bfloat16
    mesh_id = pl.DeviceIdType.MESH
    me = lax.axis_index("reg") * ndam + lax.axis_index("dam")
    slots = recv.shape[0]
    dcount = dam_out.shape[0]
    nodes = cf_ref.shape[1]
    width = GROUP * nodes
    groups = cf_ref.shape[0] // GROUP
    samples = recv.shape[1] // 3
    lands_f, lands_b = (land_f0, land_f1), (land_b0, land_b1)
    blocks = stage_f.shape

    barrier = pltpu.get_barrier_semaphore()

    def greet(step, carry):
        peer = lax.rem(me + step, n)
        pl.semaphore_signal(barrier, 1, device_id=(peer // ndam, peer % ndam),
                            device_id_type=mesh_id)
        return carry

    lax.fori_loop(1, n, greet, 0)

    def build_selectors(g, carry):
        for k in range(GROUP):
            lanes = slice(k * nodes, (k + 1) * nodes)
            cf = cf_ref[pl.ds(g * GROUP + k, 1), :]
            cd = cd_ref[pl.ds(g * GROUP + k, 1), :]
            ohtf_buf[g, :, lanes] = (
                lax.broadcasted_iota(jnp.int32, (slots, nodes), 0) == cf).astype(bf16)
            ohtd_buf[g, :, lanes] = (
                lax.broadcasted_iota(jnp.int32, (dcount, nodes), 0) == cd).astype(bf16)
        rows = pl.ds(pl.multiple_of(g * width, width), width)
        ohf_buf[rows, :] = jnp.transpose(ohtf_buf[g].astype(f32)).astype(bf16)
        ohd_buf[rows, :] = jnp.transpose(ohtd_buf[g].astype(f32)).astype(bf16)
        return carry

    lax.fori_loop(0, groups, build_selectors, 0)
    size = sp_ref.shape[0]
    across = lax.broadcasted_iota(jnp.int32, (size, size), 0)
    down = lax.broadcasted_iota(jnp.int32, (size, size), 1)
    pick_rows = (down == (across % nodes) * 3 + across // nodes).astype(bf16)
    pick_cols = (across == (down % nodes) * 3 + down // nodes).astype(bf16)
    permuted = jnp.dot(pick_rows, stiff_ref[...], preferred_element_type=f32).astype(bf16)
    sp_ref[...] = jnp.dot(permuted, pick_cols, preferred_element_type=f32).astype(bf16)
    regional = routes_ref.shape[0]
    capacity = slots // n
    first = routes_ref[:, 0:1]
    second = routes_ref[:, 1:2]
    numbers = lax.broadcasted_iota(jnp.int32, (regional, n), 1)
    hit_first = (first == numbers).astype(f32)
    hit_second = (second == numbers).astype(f32)
    earlier = (lax.broadcasted_iota(jnp.int32, (regional, regional), 1)
               < lax.broadcasted_iota(jnp.int32, (regional, regional), 0)).astype(bf16)
    counts = jnp.dot(earlier, (hit_first + hit_second).astype(bf16), preferred_element_type=f32)
    slot_first = jnp.sum(counts * hit_first, axis=1, keepdims=True).astype(jnp.int32)
    slot_second = jnp.sum(counts * hit_second, axis=1, keepdims=True).astype(jnp.int32)
    place_first = first * capacity + slot_first
    place_second = second * capacity + slot_second
    columns = lax.broadcasted_iota(jnp.int32, (regional, slots), 1)
    pair = jnp.logical_or(columns == place_first, columns == place_second).astype(f32)
    q_ref[...] = pair.astype(bf16)
    qt_ref[...] = jnp.transpose(pair).astype(bf16)
    dstep_ref[...] = jnp.transpose(
        jnp.broadcast_to(dstep_row[...], (8, dstep_row.shape[1])))[:, 0:1]
    rstep_ref[...] = jnp.transpose(
        jnp.broadcast_to(rstep_row[...], (8, rstep_row.shape[1])))[:, 0:1]
    pl.semaphore_wait(barrier, n - 1)

    def local_copy(src, dst):
        cp = pltpu.make_async_copy(src, dst, sems.at[0])
        cp.start()
        cp.wait()

    def start_exchange(stage, land, base):
        own = pltpu.make_async_copy(stage.at[me], land.at[me], sems.at[base + 2])
        own.start()

        def send(step, carry):
            peer = lax.rem(me + step, n)
            pltpu.make_async_remote_copy(
                src_ref=stage.at[peer],
                dst_ref=land.at[me],
                send_sem=sems.at[base],
                recv_sem=sems.at[base + 1],
                device_id=(peer // ndam, peer % ndam),
                device_id_type=mesh_id,
            ).start()
            return carry

        lax.fori_loop(1, n, send, 0)
        return own

    def finish_exchange(stage, land, base, own):
        everything = pltpu.make_async_remote_copy(
            src_ref=stage.at[pl.ds(0, n - 1)],
            dst_ref=land.at[pl.ds(0, n - 1)],
            send_sem=sems.at[base],
            recv_sem=sems.at[base + 1],
            device_id=(me // ndam, me % ndam),
            device_id_type=mesh_id,
        )
        everything.wait_send()
        everything.wait_recv()
        own.wait()

    def node_major(u, k):
        lo_row, hi_row = k * nodes, (k + 1) * nodes
        return jnp.concatenate(
            [u[lo_row:hi_row, c * samples:(c + 1) * samples] for c in range(3)], axis=0)

    def gather_all(select, table, out):
        for part in range(GATHER_PARTS):
            rows = slice(part * out.shape[0] // GATHER_PARTS, (part + 1) * out.shape[0] // GATHER_PARTS)
            out[rows, :] = jnp.dot(select[rows, :], table[...],
                                   preferred_element_type=f32).astype(bf16)

    def dam_side(g, carry):
        rows = pl.ds(pl.multiple_of(g * width, width), width)
        ud = ud_buf[rows, :]
        side = jnp.concatenate([node_major(ud, k) for k in range(GROUP)], axis=1)
        ssd_buf[g] = jnp.dot(sp_ref[...], side, preferred_element_type=f32)
        return carry

    def free_side(g, carry):
        rows = pl.ds(pl.multiple_of(g * width, width), width)
        uf = uf_buf[rows, :]
        ud = ud_buf[rows, :]
        forces = []
        free_all = [node_major(uf, k) for k in range(GROUP)]
        ss_all = ssd_buf[g] + jnp.dot(sp_ref[...], jnp.concatenate(free_all, axis=1),
                                      preferred_element_type=f32)
        for k in range(GROUP):
            e = g * GROUP + k
            wf = free_all[k]
            wd = node_major(ud, k)
            ss = ss_all[:, k * samples:(k + 1) * samples]
            tot = wf.astype(f32) + wd.astype(f32)
            lane = lax.broadcasted_iota(jnp.int32, tot.shape, 1)
            prev = jnp.where(lane == 0, 0.0, pltpu.roll(tot, 1, 1))
            nxt = jnp.where(lane == samples - 1, 0.0, pltpu.roll(tot, samples - 1, 1))
            accel = (nxt - 2.0 * tot) + prev
            f = sc_ref[e] * ss + mc_ref[e] * accel
            forces.append(
                jnp.concatenate([f[c * nodes:(c + 1) * nodes, :] for c in range(3)], axis=1))
        fg = jnp.concatenate(forces, axis=0)
        hi = fg.astype(bf16)
        lo = (fg - hi.astype(f32)).astype(bf16)
        hi_buf[rows, :] = hi
        lo_buf[rows, :] = lo
        both = jnp.dot(ohtf_buf[g], jnp.concatenate([hi, lo], axis=1),
                       preferred_element_type=f32)
        back[...] += both[:, :3 * samples] + both[:, 3 * samples:]
        return carry

    def dam_scatter(g, carry):
        rows = pl.ds(pl.multiple_of(g * width, width), width)
        both = jnp.dot(ohtd_buf[g], jnp.concatenate([hi_buf[rows, :], lo_buf[rows, :]], axis=1),
                       preferred_element_type=f32)
        dsum[...] += both[:, :3 * samples] + both[:, 3 * samples:]
        return carry

    hist_out[...] = hist_ref[...]
    dam_out[...] = dam_ref[...]
    for r in range(ROUNDS):
        base_f, base_b = 1 + 6 * r, 4 + 6 * r
        outgoing = jnp.dot(qt_ref[...], hist_out[...], preferred_element_type=f32).astype(bf16)
        stage_f[...] = outgoing.reshape(blocks)
        own_f = start_exchange(stage_f, lands_f[r], base_f)
        gather_all(ohd_buf, dam_out, ud_buf)
        lax.fori_loop(0, groups, dam_side, 0)
        finish_exchange(stage_f, lands_f[r], base_f, own_f)
        local_copy(lands_f[r], landv_f)
        recv[...] = landv_f[...].reshape(recv.shape)

        back[...] = jnp.zeros(back.shape, f32)
        gather_all(ohf_buf, recv, uf_buf)
        lax.fori_loop(0, groups, free_side, 0)
        stage_b[...] = back[...].reshape(blocks)
        own_b = start_exchange(stage_b, lands_b[r], base_b)
        dsum[...] = jnp.zeros(dsum.shape, f32)
        lax.fori_loop(0, groups, dam_scatter, 0)
        dam_out[...] = (dam_out[...].astype(f32) - dstep_ref[...] * dsum[...]).astype(bf16)
        finish_exchange(stage_b, lands_b[r], base_b, own_b)
        local_copy(lands_b[r], landv_b)
        ret[...] = landv_b[...].reshape(ret.shape)

        returned = ret[...]
        ret_hi = returned.astype(bf16)
        ret_lo = (returned - ret_hi.astype(f32)).astype(bf16)
        pulled = (jnp.dot(q_ref[...], ret_hi, preferred_element_type=f32)
                  + jnp.dot(q_ref[...], ret_lo, preferred_element_type=f32))
        hist_out[...] = (hist_out[...].astype(f32) - rstep_ref[...] * pulled).astype(bf16)
        if r == ROUNDS - 1:
            pulled_out[...] = pulled


def hand_over_kernel(a_ref, b_ref, c_ref, a_out, b_out, c_out, sems):
    copies = [pltpu.make_async_copy(src, dst, sems.at[i])
              for i, (src, dst) in enumerate(((a_ref, a_out), (b_ref, b_out), (c_ref, c_out)))]
    for cp in copies:
        cp.start()
    for cp in copies:
        cp.wait()


def hand_over(results):
    anywhere = pl.BlockSpec(memory_space=pl.ANY)
    return pl.pallas_call(
        hand_over_kernel,
        out_shape=tuple(jax.ShapeDtypeStruct(x.shape, x.dtype) for x in results),
        in_specs=[anywhere] * 3,
        out_specs=(anywhere,) * 3,
        scratch_shapes=[pltpu.SemaphoreType.DMA((3,))],
    )(*results)


def shards(history, routes, dam_field, conn_free, conn_dam, stiff_ref, stiff_coef,
           mass_coef, reg_step, dam_step):
    devices = lax.axis_size(("reg", "dam"))
    ndam = lax.axis_size("dam")
    row_count, row_width = history.shape
    capacity = 4 * row_count // devices
    slots = devices * capacity
    nodes = conn_free.shape[1]
    samples = row_width // 3
    smem = pl.BlockSpec(memory_space=pltpu.SMEM)
    vmem = pl.BlockSpec(memory_space=pltpu.VMEM)
    anywhere = pl.BlockSpec(memory_space=pl.ANY)
    elements = conn_free.shape[0]
    groups = conn_free.shape[0] // GROUP
    hbm_f = jax.ShapeDtypeStruct((devices, capacity, row_width), jnp.bfloat16)
    hbm_b = jax.ShapeDtypeStruct((devices, capacity, row_width), jnp.float32)
    outs = pl.pallas_call(
        functools.partial(coupling_kernel, devices, ndam),
        out_shape=(
            jax.ShapeDtypeStruct(history.shape, jnp.bfloat16),
            jax.ShapeDtypeStruct(history.shape, jnp.float32),
            jax.ShapeDtypeStruct(dam_field.shape, jnp.bfloat16),
            hbm_f, hbm_f, hbm_b, hbm_b,
        ),
        in_specs=[smem, smem] + [vmem] * 8,
        out_specs=(vmem, vmem, vmem) + (anywhere,) * 4,
        scratch_shapes=[
            pltpu.VMEM(hbm_f.shape, jnp.bfloat16),
            pltpu.VMEM(hbm_b.shape, jnp.float32),
            pltpu.VMEM(hbm_f.shape, jnp.bfloat16),
            pltpu.VMEM(hbm_b.shape, jnp.float32),
            pltpu.VMEM((slots, row_width), jnp.bfloat16),
            pltpu.VMEM((elements * nodes, row_width), jnp.bfloat16),
            pltpu.VMEM((groups, 3 * nodes, GROUP * samples), jnp.float32),
            pltpu.VMEM((elements * nodes, row_width), jnp.bfloat16),
            pltpu.VMEM((elements * nodes, row_width), jnp.bfloat16),
            pltpu.VMEM((slots, row_width), jnp.float32),
            pltpu.VMEM(dam_field.shape, jnp.float32),
            pltpu.VMEM((slots, row_width), jnp.float32),
            pltpu.VMEM((elements * nodes, slots), jnp.bfloat16),
            pltpu.VMEM((elements * nodes, dam_field.shape[0]), jnp.bfloat16),
            pltpu.VMEM((groups, slots, GROUP * nodes), jnp.bfloat16),
            pltpu.VMEM((groups, dam_field.shape[0], GROUP * nodes), jnp.bfloat16),
            pltpu.VMEM((elements * nodes, row_width), jnp.bfloat16),
            pltpu.VMEM(stiff_ref.shape, jnp.bfloat16),
            pltpu.VMEM((row_count, slots), jnp.bfloat16),
            pltpu.VMEM((slots, row_count), jnp.bfloat16),
            pltpu.VMEM((dam_field.shape[0], 1), jnp.float32),
            pltpu.VMEM((row_count, 1), jnp.float32),
            pltpu.SemaphoreType.DMA((1 + 6 * ROUNDS,)),
        ],
        compiler_params=pltpu.CompilerParams(
            collective_id=0, has_side_effects=True, vmem_limit_bytes=60 * 1024 * 1024),
    )(stiff_coef, mass_coef, history, dam_field, conn_free, conn_dam, stiff_ref,
      dam_step.reshape(1, -1), reg_step.reshape(1, -1), routes)
    return hand_over((outs[0], outs[1], outs[2]))


def solution(mesh):
    in_specs = (
        P(("reg", "dam"), None),
        P(("reg", "dam"), None),
        P(("reg", "dam"), None),
        P(("reg", "dam"), None),
        P(("reg", "dam"), None),
        P(),
        P(("reg", "dam")),
        P(("reg", "dam")),
        P(("reg", "dam")),
        P(("reg", "dam")),
    )
    out_specs = (P(("reg", "dam"), None), P(("reg", "dam"), None), P(("reg", "dam"), None))
    return jax.shard_map(shards, mesh=mesh, in_specs=in_specs, out_specs=out_specs, check_vma=False)
```

```python
import functools

import jax
import jax.numpy as jnp
from jax import lax
from jax.experimental import pallas as pl
from jax.experimental.pallas import tpu as pltpu
from jax.sharding import PartitionSpec as P

ROUNDS = 2
GROUP = 4
GATHER_PARTS = 4


def coupling_kernel(n, ndam, sc_ref, mc_ref, hist_ref, dam_ref, cf_ref, cd_ref, stiff_ref,
                    dstep_row, rstep_row, routes_ref,
                    hist_out, pulled_out, dam_out,
                    land_f0, land_f1, land_b0, land_b1,
                    stage_f, stage_b, landv_f, landv_b,
                    recv, ud_buf, ssd_buf, hi_buf, lo_buf, back, dsum, ret,
                    ohf_buf, ohd_buf, ohtf_buf, ohtd_buf, uf_buf, sp_ref, q_ref, qt_ref, dstep_ref, rstep_ref,
                    sems):
    f32, bf16 = jnp.float32, jnp.bfloat16
    mesh_id = pl.DeviceIdType.MESH
    me = lax.axis_index("reg") * ndam + lax.axis_index("dam")
    slots = recv.shape[0]
    dcount = dam_out.shape[0]
    nodes = cf_ref.shape[1]
    width = GROUP * nodes
    groups = cf_ref.shape[0] // GROUP
    samples = recv.shape[1] // 3
    lands_f, lands_b = (land_f0, land_f1), (land_b0, land_b1)
    blocks = stage_f.shape

    barrier = pltpu.get_barrier_semaphore()

    def greet(step, carry):
        peer = lax.rem(me + step, n)
        pl.semaphore_signal(barrier, 1, device_id=(peer // ndam, peer % ndam),
                            device_id_type=mesh_id)
        return carry

    lax.fori_loop(1, n, greet, 0)

    def build_selectors(g, carry):
        for k in range(GROUP):
            lanes = slice(k * nodes, (k + 1) * nodes)
            cf = cf_ref[pl.ds(g * GROUP + k, 1), :]
            cd = cd_ref[pl.ds(g * GROUP + k, 1), :]
            ohtf_buf[g, :, lanes] = (
                lax.broadcasted_iota(jnp.int32, (slots, nodes), 0) == cf).astype(bf16)
            ohtd_buf[g, :, lanes] = (
                lax.broadcasted_iota(jnp.int32, (dcount, nodes), 0) == cd).astype(bf16)
        rows = pl.ds(pl.multiple_of(g * width, width), width)
        ohf_buf[rows, :] = jnp.transpose(ohtf_buf[g].astype(f32)).astype(bf16)
        ohd_buf[rows, :] = jnp.transpose(ohtd_buf[g].astype(f32)).astype(bf16)
        return carry

    lax.fori_loop(0, groups, build_selectors, 0)
    size = sp_ref.shape[0]
    across = lax.broadcasted_iota(jnp.int32, (size, size), 0)
    down = lax.broadcasted_iota(jnp.int32, (size, size), 1)
    pick_rows = (down == (across % nodes) * 3 + across // nodes).astype(bf16)
    pick_cols = (across == (down % nodes) * 3 + down // nodes).astype(bf16)
    permuted = jnp.dot(pick_rows, stiff_ref[...], preferred_element_type=f32).astype(bf16)
    sp_ref[...] = jnp.dot(permuted, pick_cols, preferred_element_type=f32).astype(bf16)
    regional = routes_ref.shape[1]
    capacity = slots // n
    first = routes_ref[0:1, :]
    second = routes_ref[1:2, :]
    numbers = lax.broadcasted_iota(jnp.int32, (n, regional), 0)
    hit_first = (first == numbers).astype(f32)
    hit_second = (second == numbers).astype(f32)
    earlier = (lax.broadcasted_iota(jnp.int32, (regional, regional), 0)
               < lax.broadcasted_iota(jnp.int32, (regional, regional), 1)).astype(bf16)
    counts = jnp.dot((hit_first + hit_second).astype(bf16), earlier, preferred_element_type=f32)
    slot_first = jnp.sum(counts * hit_first, axis=0, keepdims=True).astype(jnp.int32)
    slot_second = jnp.sum(counts * hit_second, axis=0, keepdims=True).astype(jnp.int32)
    place_first = first * capacity + slot_first
    place_second = second * capacity + slot_second
    positions = lax.broadcasted_iota(jnp.int32, (slots, regional), 0)
    pair = jnp.logical_or(positions == place_first, positions == place_second).astype(f32)
    qt_ref[...] = pair.astype(bf16)
    q_ref[...] = jnp.transpose(pair).astype(bf16)
    dstep_ref[...] = jnp.transpose(
        jnp.broadcast_to(dstep_row[...], (8, dstep_row.shape[1])))[:, 0:1]
    rstep_ref[...] = jnp.transpose(
        jnp.broadcast_to(rstep_row[...], (8, rstep_row.shape[1])))[:, 0:1]
    pl.semaphore_wait(barrier, n - 1)

    def local_copy(src, dst):
        cp = pltpu.make_async_copy(src, dst, sems.at[0])
        cp.start()
        cp.wait()

    def start_exchange(stage, land, base):
        own = pltpu.make_async_copy(stage.at[me], land.at[me], sems.at[base + 2])
        own.start()

        def send(step, carry):
            peer = lax.rem(me + step, n)
            pltpu.make_async_remote_copy(
                src_ref=stage.at[peer],
                dst_ref=land.at[me],
                send_sem=sems.at[base],
                recv_sem=sems.at[base + 1],
                device_id=(peer // ndam, peer % ndam),
                device_id_type=mesh_id,
            ).start()
            return carry

        lax.fori_loop(1, n, send, 0)
        return own

    def finish_exchange(stage, land, base, own):
        everything = pltpu.make_async_remote_copy(
            src_ref=stage.at[pl.ds(0, n - 1)],
            dst_ref=land.at[pl.ds(0, n - 1)],
            send_sem=sems.at[base],
            recv_sem=sems.at[base + 1],
            device_id=(me // ndam, me % ndam),
            device_id_type=mesh_id,
        )
        everything.wait_send()
        everything.wait_recv()
        own.wait()

    def node_major(u, k):
        lo_row, hi_row = k * nodes, (k + 1) * nodes
        return jnp.concatenate(
            [u[lo_row:hi_row, c * samples:(c + 1) * samples] for c in range(3)], axis=0)

    def gather_all(select, table, out):
        for part in range(GATHER_PARTS):
            rows = slice(part * out.shape[0] // GATHER_PARTS, (part + 1) * out.shape[0] // GATHER_PARTS)
            out[rows, :] = jnp.dot(select[rows, :], table[...],
                                   preferred_element_type=f32).astype(bf16)

    def dam_side(g, carry):
        rows = pl.ds(pl.multiple_of(g * width, width), width)
        ud = ud_buf[rows, :]
        side = jnp.concatenate([node_major(ud, k) for k in range(GROUP)], axis=1)
        ssd_buf[g] = jnp.dot(sp_ref[...], side, preferred_element_type=f32)
        return carry

    def free_side(g, carry):
        rows = pl.ds(pl.multiple_of(g * width, width), width)
        uf = uf_buf[rows, :]
        ud = ud_buf[rows, :]
        forces = []
        free_all = [node_major(uf, k) for k in range(GROUP)]
        ss_all = ssd_buf[g] + jnp.dot(sp_ref[...], jnp.concatenate(free_all, axis=1),
                                      preferred_element_type=f32)
        for k in range(GROUP):
            e = g * GROUP + k
            wf = free_all[k]
            wd = node_major(ud, k)
            ss = ss_all[:, k * samples:(k + 1) * samples]
            tot = wf.astype(f32) + wd.astype(f32)
            lane = lax.broadcasted_iota(jnp.int32, tot.shape, 1)
            prev = jnp.where(lane == 0, 0.0, pltpu.roll(tot, 1, 1))
            nxt = jnp.where(lane == samples - 1, 0.0, pltpu.roll(tot, samples - 1, 1))
            accel = (nxt - 2.0 * tot) + prev
            f = sc_ref[e] * ss + mc_ref[e] * accel
            forces.append(
                jnp.concatenate([f[c * nodes:(c + 1) * nodes, :] for c in range(3)], axis=1))
        fg = jnp.concatenate(forces, axis=0)
        hi = fg.astype(bf16)
        lo = (fg - hi.astype(f32)).astype(bf16)
        hi_buf[rows, :] = hi
        lo_buf[rows, :] = lo
        both = jnp.dot(ohtf_buf[g], jnp.concatenate([hi, lo], axis=1),
                       preferred_element_type=f32)
        back[...] += both[:, :3 * samples] + both[:, 3 * samples:]
        return carry

    def dam_scatter(g, carry):
        rows = pl.ds(pl.multiple_of(g * width, width), width)
        both = jnp.dot(ohtd_buf[g], jnp.concatenate([hi_buf[rows, :], lo_buf[rows, :]], axis=1),
                       preferred_element_type=f32)
        dsum[...] += both[:, :3 * samples] + both[:, 3 * samples:]
        return carry

    hist_out[...] = hist_ref[...]
    dam_out[...] = dam_ref[...]
    for r in range(ROUNDS):
        base_f, base_b = 1 + 6 * r, 4 + 6 * r
        outgoing = jnp.dot(qt_ref[...], hist_out[...], preferred_element_type=f32).astype(bf16)
        stage_f[...] = outgoing.reshape(blocks)
        own_f = start_exchange(stage_f, lands_f[r], base_f)
        gather_all(ohd_buf, dam_out, ud_buf)
        lax.fori_loop(0, groups, dam_side, 0)
        finish_exchange(stage_f, lands_f[r], base_f, own_f)
        local_copy(lands_f[r], landv_f)
        recv[...] = landv_f[...].reshape(recv.shape)

        back[...] = jnp.zeros(back.shape, f32)
        gather_all(ohf_buf, recv, uf_buf)
        lax.fori_loop(0, groups, free_side, 0)
        stage_b[...] = back[...].reshape(blocks)
        own_b = start_exchange(stage_b, lands_b[r], base_b)
        dsum[...] = jnp.zeros(dsum.shape, f32)
        lax.fori_loop(0, groups, dam_scatter, 0)
        dam_out[...] = (dam_out[...].astype(f32) - dstep_ref[...] * dsum[...]).astype(bf16)
        finish_exchange(stage_b, lands_b[r], base_b, own_b)
        local_copy(lands_b[r], landv_b)
        ret[...] = landv_b[...].reshape(ret.shape)

        returned = ret[...]
        ret_hi = returned.astype(bf16)
        ret_lo = (returned - ret_hi.astype(f32)).astype(bf16)
        pulled = (jnp.dot(q_ref[...], ret_hi, preferred_element_type=f32)
                  + jnp.dot(q_ref[...], ret_lo, preferred_element_type=f32))
        hist_out[...] = (hist_out[...].astype(f32) - rstep_ref[...] * pulled).astype(bf16)
        if r == ROUNDS - 1:
            pulled_out[...] = pulled


def shards(history, routes, dam_field, conn_free, conn_dam, stiff_ref, stiff_coef,
           mass_coef, reg_step, dam_step):
    devices = lax.axis_size(("reg", "dam"))
    ndam = lax.axis_size("dam")
    row_count, row_width = history.shape
    capacity = 4 * row_count // devices
    slots = devices * capacity
    nodes = conn_free.shape[1]
    samples = row_width // 3
    smem = pl.BlockSpec(memory_space=pltpu.SMEM)
    vmem = pl.BlockSpec(memory_space=pltpu.VMEM)
    anywhere = pl.BlockSpec(memory_space=pl.ANY)
    elements = conn_free.shape[0]
    groups = conn_free.shape[0] // GROUP
    hbm_f = jax.ShapeDtypeStruct((devices, capacity, row_width), jnp.bfloat16)
    hbm_b = jax.ShapeDtypeStruct((devices, capacity, row_width), jnp.float32)
    outs = pl.pallas_call(
        functools.partial(coupling_kernel, devices, ndam),
        out_shape=(
            jax.ShapeDtypeStruct(history.shape, jnp.bfloat16),
            jax.ShapeDtypeStruct(history.shape, jnp.float32),
            jax.ShapeDtypeStruct(dam_field.shape, jnp.bfloat16),
            hbm_f, hbm_f, hbm_b, hbm_b,
        ),
        in_specs=[smem, smem] + [vmem] * 8,
        out_specs=(vmem, vmem, vmem) + (anywhere,) * 4,
        scratch_shapes=[
            pltpu.VMEM(hbm_f.shape, jnp.bfloat16),
            pltpu.VMEM(hbm_b.shape, jnp.float32),
            pltpu.VMEM(hbm_f.shape, jnp.bfloat16),
            pltpu.VMEM(hbm_b.shape, jnp.float32),
            pltpu.VMEM((slots, row_width), jnp.bfloat16),
            pltpu.VMEM((elements * nodes, row_width), jnp.bfloat16),
            pltpu.VMEM((groups, 3 * nodes, GROUP * samples), jnp.float32),
            pltpu.VMEM((elements * nodes, row_width), jnp.bfloat16),
            pltpu.VMEM((elements * nodes, row_width), jnp.bfloat16),
            pltpu.VMEM((slots, row_width), jnp.float32),
            pltpu.VMEM(dam_field.shape, jnp.float32),
            pltpu.VMEM((slots, row_width), jnp.float32),
            pltpu.VMEM((elements * nodes, slots), jnp.bfloat16),
            pltpu.VMEM((elements * nodes, dam_field.shape[0]), jnp.bfloat16),
            pltpu.VMEM((groups, slots, GROUP * nodes), jnp.bfloat16),
            pltpu.VMEM((groups, dam_field.shape[0], GROUP * nodes), jnp.bfloat16),
            pltpu.VMEM((elements * nodes, row_width), jnp.bfloat16),
            pltpu.VMEM(stiff_ref.shape, jnp.bfloat16),
            pltpu.VMEM((row_count, slots), jnp.bfloat16),
            pltpu.VMEM((slots, row_count), jnp.bfloat16),
            pltpu.VMEM((dam_field.shape[0], 1), jnp.float32),
            pltpu.VMEM((row_count, 1), jnp.float32),
            pltpu.SemaphoreType.DMA((1 + 6 * ROUNDS,)),
        ],
        compiler_params=pltpu.CompilerParams(
            collective_id=0, has_side_effects=True, vmem_limit_bytes=60 * 1024 * 1024),
    )(stiff_coef, mass_coef, history, dam_field, conn_free, conn_dam, stiff_ref,
      dam_step.reshape(1, -1), reg_step.reshape(1, -1), jnp.transpose(routes))
    return (outs[0], outs[1], outs[2])


def solution(mesh):
    in_specs = (
        P(("reg", "dam"), None),
        P(("reg", "dam"), None),
        P(("reg", "dam"), None),
        P(("reg", "dam"), None),
        P(("reg", "dam"), None),
        P(),
        P(("reg", "dam")),
        P(("reg", "dam")),
        P(("reg", "dam")),
        P(("reg", "dam")),
    )
    out_specs = (P(("reg", "dam"), None), P(("reg", "dam"), None), P(("reg", "dam"), None))
    return jax.shard_map(shards, mesh=mesh, in_specs=in_specs, out_specs=out_specs, check_vma=False)
```

```python
import functools

import jax
import jax.numpy as jnp
from jax import lax
from jax.experimental import pallas as pl
from jax.experimental.pallas import tpu as pltpu
from jax.sharding import PartitionSpec as P

ROUNDS = 2
GROUP = 8
GATHER_PARTS = 4


def coupling_kernel(n, ndam, sc_ref, mc_ref, hist_ref, dam_ref, cf_ref, cd_ref, stiff_ref,
                    dstep_row, rstep_row, routes_ref,
                    hist_out, pulled_out, dam_out,
                    land_f0, land_f1, land_b0, land_b1,
                    stage_f, stage_b, landv_f, landv_b,
                    recv, ud_buf, ssd_buf, hi_buf, lo_buf, back, dsum, ret,
                    ohf_buf, ohd_buf, ohtf_buf, ohtd_buf, uf_buf, sp_ref, q_ref, qt_ref, dstep_ref, rstep_ref,
                    sems):
    f32, bf16 = jnp.float32, jnp.bfloat16
    mesh_id = pl.DeviceIdType.MESH
    me = lax.axis_index("reg") * ndam + lax.axis_index("dam")
    slots = recv.shape[0]
    dcount = dam_out.shape[0]
    nodes = cf_ref.shape[1]
    width = GROUP * nodes
    groups = cf_ref.shape[0] // GROUP
    samples = recv.shape[1] // 3
    lands_f, lands_b = (land_f0, land_f1), (land_b0, land_b1)
    blocks = stage_f.shape

    barrier = pltpu.get_barrier_semaphore()

    def greet(step, carry):
        peer = lax.rem(me + step, n)
        pl.semaphore_signal(barrier, 1, device_id=(peer // ndam, peer % ndam),
                            device_id_type=mesh_id)
        return carry

    lax.fori_loop(1, n, greet, 0)

    def build_selectors(g, carry):
        for k in range(GROUP):
            lanes = slice(k * nodes, (k + 1) * nodes)
            cf = cf_ref[pl.ds(g * GROUP + k, 1), :]
            cd = cd_ref[pl.ds(g * GROUP + k, 1), :]
            ohtf_buf[g, :, lanes] = (
                lax.broadcasted_iota(jnp.int32, (slots, nodes), 0) == cf).astype(bf16)
            ohtd_buf[g, :, lanes] = (
                lax.broadcasted_iota(jnp.int32, (dcount, nodes), 0) == cd).astype(bf16)
        rows = pl.ds(pl.multiple_of(g * width, width), width)
        ohf_buf[rows, :] = jnp.transpose(ohtf_buf[g].astype(f32)).astype(bf16)
        ohd_buf[rows, :] = jnp.transpose(ohtd_buf[g].astype(f32)).astype(bf16)
        return carry

    lax.fori_loop(0, groups, build_selectors, 0)
    size = sp_ref.shape[0]
    across = lax.broadcasted_iota(jnp.int32, (size, size), 0)
    down = lax.broadcasted_iota(jnp.int32, (size, size), 1)
    pick_rows = (down == (across % nodes) * 3 + across // nodes).astype(bf16)
    pick_cols = (across == (down % nodes) * 3 + down // nodes).astype(bf16)
    permuted = jnp.dot(pick_rows, stiff_ref[...], preferred_element_type=f32).astype(bf16)
    sp_ref[...] = jnp.dot(permuted, pick_cols, preferred_element_type=f32).astype(bf16)
    regional = routes_ref.shape[1]
    capacity = slots // n
    first = routes_ref[0:1, :]
    second = routes_ref[1:2, :]
    numbers = lax.broadcasted_iota(jnp.int32, (n, regional), 0)
    hit_first = (first == numbers).astype(f32)
    hit_second = (second == numbers).astype(f32)
    earlier = (lax.broadcasted_iota(jnp.int32, (regional, regional), 0)
               < lax.broadcasted_iota(jnp.int32, (regional, regional), 1)).astype(bf16)
    counts = jnp.dot((hit_first + hit_second).astype(bf16), earlier, preferred_element_type=f32)
    slot_first = jnp.sum(counts * hit_first, axis=0, keepdims=True).astype(jnp.int32)
    slot_second = jnp.sum(counts * hit_second, axis=0, keepdims=True).astype(jnp.int32)
    place_first = first * capacity + slot_first
    place_second = second * capacity + slot_second
    positions = lax.broadcasted_iota(jnp.int32, (slots, regional), 0)
    pair = jnp.logical_or(positions == place_first, positions == place_second).astype(f32)
    qt_ref[...] = pair.astype(bf16)
    q_ref[...] = jnp.transpose(pair).astype(bf16)
    dstep_ref[...] = jnp.transpose(
        jnp.broadcast_to(dstep_row[...], (8, dstep_row.shape[1])))[:, 0:1]
    rstep_ref[...] = jnp.transpose(
        jnp.broadcast_to(rstep_row[...], (8, rstep_row.shape[1])))[:, 0:1]
    pl.semaphore_wait(barrier, n - 1)

    def local_copy(src, dst):
        cp = pltpu.make_async_copy(src, dst, sems.at[0])
        cp.start()
        cp.wait()

    def start_exchange(stage, land, base):
        own = pltpu.make_async_copy(stage.at[me], land.at[me], sems.at[base + 2])
        own.start()

        def send(step, carry):
            peer = lax.rem(me + step, n)
            pltpu.make_async_remote_copy(
                src_ref=stage.at[peer],
                dst_ref=land.at[me],
                send_sem=sems.at[base],
                recv_sem=sems.at[base + 1],
                device_id=(peer // ndam, peer % ndam),
                device_id_type=mesh_id,
            ).start()
            return carry

        lax.fori_loop(1, n, send, 0)
        return own

    def finish_exchange(stage, land, base, own):
        everything = pltpu.make_async_remote_copy(
            src_ref=stage.at[pl.ds(0, n - 1)],
            dst_ref=land.at[pl.ds(0, n - 1)],
            send_sem=sems.at[base],
            recv_sem=sems.at[base + 1],
            device_id=(me // ndam, me % ndam),
            device_id_type=mesh_id,
        )
        everything.wait_send()
        everything.wait_recv()
        own.wait()

    def node_major(u, k):
        lo_row, hi_row = k * nodes, (k + 1) * nodes
        return jnp.concatenate(
            [u[lo_row:hi_row, c * samples:(c + 1) * samples] for c in range(3)], axis=0)

    def gather_all(select, table, out):
        for part in range(GATHER_PARTS):
            rows = slice(part * out.shape[0] // GATHER_PARTS, (part + 1) * out.shape[0] // GATHER_PARTS)
            out[rows, :] = jnp.dot(select[rows, :], table[...],
                                   preferred_element_type=f32).astype(bf16)

    def dam_side(g, carry):
        rows = pl.ds(pl.multiple_of(g * width, width), width)
        ud = ud_buf[rows, :]
        side = jnp.concatenate([node_major(ud, k) for k in range(GROUP)], axis=1)
        ssd_buf[g] = jnp.dot(sp_ref[...], side, preferred_element_type=f32)
        return carry

    def free_side(g, carry):
        rows = pl.ds(pl.multiple_of(g * width, width), width)
        uf = uf_buf[rows, :]
        ud = ud_buf[rows, :]
        forces = []
        free_all = [node_major(uf, k) for k in range(GROUP)]
        ss_all = ssd_buf[g] + jnp.dot(sp_ref[...], jnp.concatenate(free_all, axis=1),
                                      preferred_element_type=f32)
        for k in range(GROUP):
            e = g * GROUP + k
            wf = free_all[k]
            wd = node_major(ud, k)
            ss = ss_all[:, k * samples:(k + 1) * samples]
            tot = wf.astype(f32) + wd.astype(f32)
            lane = lax.broadcasted_iota(jnp.int32, tot.shape, 1)
            prev = jnp.where(lane == 0, 0.0, pltpu.roll(tot, 1, 1))
            nxt = jnp.where(lane == samples - 1, 0.0, pltpu.roll(tot, samples - 1, 1))
            accel = (nxt - 2.0 * tot) + prev
            f = sc_ref[e] * ss + mc_ref[e] * accel
            forces.append(
                jnp.concatenate([f[c * nodes:(c + 1) * nodes, :] for c in range(3)], axis=1))
        fg = jnp.concatenate(forces, axis=0)
        hi = fg.astype(bf16)
        lo = (fg - hi.astype(f32)).astype(bf16)
        hi_buf[rows, :] = hi
        lo_buf[rows, :] = lo
        both = jnp.dot(ohtf_buf[g], jnp.concatenate([hi, lo], axis=1),
                       preferred_element_type=f32)
        back[...] += both[:, :3 * samples] + both[:, 3 * samples:]
        return carry

    def dam_scatter(g, carry):
        rows = pl.ds(pl.multiple_of(g * width, width), width)
        both = jnp.dot(ohtd_buf[g], jnp.concatenate([hi_buf[rows, :], lo_buf[rows, :]], axis=1),
                       preferred_element_type=f32)
        dsum[...] += both[:, :3 * samples] + both[:, 3 * samples:]
        return carry

    hist_out[...] = hist_ref[...]
    dam_out[...] = dam_ref[...]
    for r in range(ROUNDS):
        base_f, base_b = 1 + 6 * r, 4 + 6 * r
        outgoing = jnp.dot(qt_ref[...], hist_out[...], preferred_element_type=f32).astype(bf16)
        stage_f[...] = outgoing.reshape(blocks)
        own_f = start_exchange(stage_f, lands_f[r], base_f)
        gather_all(ohd_buf, dam_out, ud_buf)
        lax.fori_loop(0, groups, dam_side, 0)
        finish_exchange(stage_f, lands_f[r], base_f, own_f)
        local_copy(lands_f[r], landv_f)
        recv[...] = landv_f[...].reshape(recv.shape)

        back[...] = jnp.zeros(back.shape, f32)
        gather_all(ohf_buf, recv, uf_buf)
        lax.fori_loop(0, groups, free_side, 0)
        stage_b[...] = back[...].reshape(blocks)
        own_b = start_exchange(stage_b, lands_b[r], base_b)
        dsum[...] = jnp.zeros(dsum.shape, f32)
        lax.fori_loop(0, groups, dam_scatter, 0)
        dam_out[...] = (dam_out[...].astype(f32) - dstep_ref[...] * dsum[...]).astype(bf16)
        finish_exchange(stage_b, lands_b[r], base_b, own_b)
        local_copy(lands_b[r], landv_b)
        ret[...] = landv_b[...].reshape(ret.shape)

        returned = ret[...]
        ret_hi = returned.astype(bf16)
        ret_lo = (returned - ret_hi.astype(f32)).astype(bf16)
        pulled = (jnp.dot(q_ref[...], ret_hi, preferred_element_type=f32)
                  + jnp.dot(q_ref[...], ret_lo, preferred_element_type=f32))
        hist_out[...] = (hist_out[...].astype(f32) - rstep_ref[...] * pulled).astype(bf16)
        if r == ROUNDS - 1:
            pulled_out[...] = pulled


def shards(history, routes, dam_field, conn_free, conn_dam, stiff_ref, stiff_coef,
           mass_coef, reg_step, dam_step):
    devices = lax.axis_size(("reg", "dam"))
    ndam = lax.axis_size("dam")
    row_count, row_width = history.shape
    capacity = 4 * row_count // devices
    slots = devices * capacity
    nodes = conn_free.shape[1]
    samples = row_width // 3
    smem = pl.BlockSpec(memory_space=pltpu.SMEM)
    vmem = pl.BlockSpec(memory_space=pltpu.VMEM)
    anywhere = pl.BlockSpec(memory_space=pl.ANY)
    elements = conn_free.shape[0]
    groups = conn_free.shape[0] // GROUP
    hbm_f = jax.ShapeDtypeStruct((devices, capacity, row_width), jnp.bfloat16)
    hbm_b = jax.ShapeDtypeStruct((devices, capacity, row_width), jnp.float32)
    outs = pl.pallas_call(
        functools.partial(coupling_kernel, devices, ndam),
        out_shape=(
            jax.ShapeDtypeStruct(history.shape, jnp.bfloat16),
            jax.ShapeDtypeStruct(history.shape, jnp.float32),
            jax.ShapeDtypeStruct(dam_field.shape, jnp.bfloat16),
            hbm_f, hbm_f, hbm_b, hbm_b,
        ),
        in_specs=[smem, smem] + [vmem] * 8,
        out_specs=(vmem, vmem, vmem) + (anywhere,) * 4,
        scratch_shapes=[
            pltpu.VMEM(hbm_f.shape, jnp.bfloat16),
            pltpu.VMEM(hbm_b.shape, jnp.float32),
            pltpu.VMEM(hbm_f.shape, jnp.bfloat16),
            pltpu.VMEM(hbm_b.shape, jnp.float32),
            pltpu.VMEM((slots, row_width), jnp.bfloat16),
            pltpu.VMEM((elements * nodes, row_width), jnp.bfloat16),
            pltpu.VMEM((groups, 3 * nodes, GROUP * samples), jnp.float32),
            pltpu.VMEM((elements * nodes, row_width), jnp.bfloat16),
            pltpu.VMEM((elements * nodes, row_width), jnp.bfloat16),
            pltpu.VMEM((slots, row_width), jnp.float32),
            pltpu.VMEM(dam_field.shape, jnp.float32),
            pltpu.VMEM((slots, row_width), jnp.float32),
            pltpu.VMEM((elements * nodes, slots), jnp.bfloat16),
            pltpu.VMEM((elements * nodes, dam_field.shape[0]), jnp.bfloat16),
            pltpu.VMEM((groups, slots, GROUP * nodes), jnp.bfloat16),
            pltpu.VMEM((groups, dam_field.shape[0], GROUP * nodes), jnp.bfloat16),
            pltpu.VMEM((elements * nodes, row_width), jnp.bfloat16),
            pltpu.VMEM(stiff_ref.shape, jnp.bfloat16),
            pltpu.VMEM((row_count, slots), jnp.bfloat16),
            pltpu.VMEM((slots, row_count), jnp.bfloat16),
            pltpu.VMEM((dam_field.shape[0], 1), jnp.float32),
            pltpu.VMEM((row_count, 1), jnp.float32),
            pltpu.SemaphoreType.DMA((1 + 6 * ROUNDS,)),
        ],
        compiler_params=pltpu.CompilerParams(
            collective_id=0, has_side_effects=True, vmem_limit_bytes=60 * 1024 * 1024),
    )(stiff_coef, mass_coef, history, dam_field, conn_free, conn_dam, stiff_ref,
      dam_step.reshape(1, -1), reg_step.reshape(1, -1), jnp.transpose(routes))
    return (outs[0], outs[1], outs[2])


def solution(mesh):
    in_specs = (
        P(("reg", "dam"), None),
        P(("reg", "dam"), None),
        P(("reg", "dam"), None),
        P(("reg", "dam"), None),
        P(("reg", "dam"), None),
        P(),
        P(("reg", "dam")),
        P(("reg", "dam")),
        P(("reg", "dam")),
        P(("reg", "dam")),
    )
    out_specs = (P(("reg", "dam"), None), P(("reg", "dam"), None), P(("reg", "dam"), None))
    return jax.shard_map(shards, mesh=mesh, in_specs=in_specs, out_specs=out_specs, check_vma=False)
```

```python
import functools

import jax
import jax.numpy as jnp
from jax import lax
from jax.experimental import pallas as pl
from jax.experimental.pallas import tpu as pltpu
from jax.sharding import PartitionSpec as P

ROUNDS = 2
GROUP = 16
GATHER_PARTS = 4


def coupling_kernel(n, ndam, sc_ref, mc_ref, hist_ref, dam_ref, cf_ref, cd_ref, stiff_ref,
                    dstep_row, rstep_row, routes_ref,
                    hist_out, pulled_out, dam_out,
                    land_f0, land_f1, land_b0, land_b1,
                    stage_f, stage_b, landv_f, landv_b,
                    recv, ud_buf, ssd_buf, hi_buf, lo_buf, back, dsum, ret,
                    ohf_buf, ohd_buf, ohtf_buf, ohtd_buf, uf_buf, sp_ref, q_ref, qt_ref, dstep_ref, rstep_ref,
                    sems):
    f32, bf16 = jnp.float32, jnp.bfloat16
    mesh_id = pl.DeviceIdType.MESH
    me = lax.axis_index("reg") * ndam + lax.axis_index("dam")
    slots = recv.shape[0]
    dcount = dam_out.shape[0]
    nodes = cf_ref.shape[1]
    width = GROUP * nodes
    groups = cf_ref.shape[0] // GROUP
    samples = recv.shape[1] // 3
    lands_f, lands_b = (land_f0, land_f1), (land_b0, land_b1)
    blocks = stage_f.shape

    barrier = pltpu.get_barrier_semaphore()

    def greet(step, carry):
        peer = lax.rem(me + step, n)
        pl.semaphore_signal(barrier, 1, device_id=(peer // ndam, peer % ndam),
                            device_id_type=mesh_id)
        return carry

    lax.fori_loop(1, n, greet, 0)

    def build_selectors(g, carry):
        for k in range(GROUP):
            lanes = slice(k * nodes, (k + 1) * nodes)
            cf = cf_ref[pl.ds(g * GROUP + k, 1), :]
            cd = cd_ref[pl.ds(g * GROUP + k, 1), :]
            ohtf_buf[g, :, lanes] = (
                lax.broadcasted_iota(jnp.int32, (slots, nodes), 0) == cf).astype(bf16)
            ohtd_buf[g, :, lanes] = (
                lax.broadcasted_iota(jnp.int32, (dcount, nodes), 0) == cd).astype(bf16)
        rows = pl.ds(pl.multiple_of(g * width, width), width)
        ohf_buf[rows, :] = jnp.transpose(ohtf_buf[g].astype(f32)).astype(bf16)
        ohd_buf[rows, :] = jnp.transpose(ohtd_buf[g].astype(f32)).astype(bf16)
        return carry

    lax.fori_loop(0, groups, build_selectors, 0)
    size = sp_ref.shape[0]
    across = lax.broadcasted_iota(jnp.int32, (size, size), 0)
    down = lax.broadcasted_iota(jnp.int32, (size, size), 1)
    pick_rows = (down == (across % nodes) * 3 + across // nodes).astype(bf16)
    pick_cols = (across == (down % nodes) * 3 + down // nodes).astype(bf16)
    permuted = jnp.dot(pick_rows, stiff_ref[...], preferred_element_type=f32).astype(bf16)
    sp_ref[...] = jnp.dot(permuted, pick_cols, preferred_element_type=f32).astype(bf16)
    regional = routes_ref.shape[1]
    capacity = slots // n
    first = routes_ref[0:1, :]
    second = routes_ref[1:2, :]
    numbers = lax.broadcasted_iota(jnp.int32, (n, regional), 0)
    hit_first = (first == numbers).astype(f32)
    hit_second = (second == numbers).astype(f32)
    earlier = (lax.broadcasted_iota(jnp.int32, (regional, regional), 0)
               < lax.broadcasted_iota(jnp.int32, (regional, regional), 1)).astype(bf16)
    counts = jnp.dot((hit_first + hit_second).astype(bf16), earlier, preferred_element_type=f32)
    slot_first = jnp.sum(counts * hit_first, axis=0, keepdims=True).astype(jnp.int32)
    slot_second = jnp.sum(counts * hit_second, axis=0, keepdims=True).astype(jnp.int32)
    place_first = first * capacity + slot_first
    place_second = second * capacity + slot_second
    positions = lax.broadcasted_iota(jnp.int32, (slots, regional), 0)
    pair = jnp.logical_or(positions == place_first, positions == place_second).astype(f32)
    qt_ref[...] = pair.astype(bf16)
    q_ref[...] = jnp.transpose(pair).astype(bf16)
    dstep_ref[...] = jnp.transpose(
        jnp.broadcast_to(dstep_row[...], (8, dstep_row.shape[1])))[:, 0:1]
    rstep_ref[...] = jnp.transpose(
        jnp.broadcast_to(rstep_row[...], (8, rstep_row.shape[1])))[:, 0:1]
    pl.semaphore_wait(barrier, n - 1)

    def local_copy(src, dst):
        cp = pltpu.make_async_copy(src, dst, sems.at[0])
        cp.start()
        cp.wait()

    def start_exchange(stage, land, base):
        own = pltpu.make_async_copy(stage.at[me], land.at[me], sems.at[base + 2])
        own.start()

        def send(step, carry):
            peer = lax.rem(me + step, n)
            pltpu.make_async_remote_copy(
                src_ref=stage.at[peer],
                dst_ref=land.at[me],
                send_sem=sems.at[base],
                recv_sem=sems.at[base + 1],
                device_id=(peer // ndam, peer % ndam),
                device_id_type=mesh_id,
            ).start()
            return carry

        lax.fori_loop(1, n, send, 0)
        return own

    def finish_exchange(stage, land, base, own):
        everything = pltpu.make_async_remote_copy(
            src_ref=stage.at[pl.ds(0, n - 1)],
            dst_ref=land.at[pl.ds(0, n - 1)],
            send_sem=sems.at[base],
            recv_sem=sems.at[base + 1],
            device_id=(me // ndam, me % ndam),
            device_id_type=mesh_id,
        )
        everything.wait_send()
        everything.wait_recv()
        own.wait()

    def node_major(u, k):
        lo_row, hi_row = k * nodes, (k + 1) * nodes
        return jnp.concatenate(
            [u[lo_row:hi_row, c * samples:(c + 1) * samples] for c in range(3)], axis=0)

    def gather_all(select, table, out):
        for part in range(GATHER_PARTS):
            rows = slice(part * out.shape[0] // GATHER_PARTS, (part + 1) * out.shape[0] // GATHER_PARTS)
            out[rows, :] = jnp.dot(select[rows, :], table[...],
                                   preferred_element_type=f32).astype(bf16)

    def dam_side(g, carry):
        rows = pl.ds(pl.multiple_of(g * width, width), width)
        ud = ud_buf[rows, :]
        side = jnp.concatenate([node_major(ud, k) for k in range(GROUP)], axis=1)
        ssd_buf[g] = jnp.dot(sp_ref[...], side, preferred_element_type=f32)
        return carry

    def free_side(g, carry):
        rows = pl.ds(pl.multiple_of(g * width, width), width)
        uf = uf_buf[rows, :]
        ud = ud_buf[rows, :]
        forces = []
        free_all = [node_major(uf, k) for k in range(GROUP)]
        ss_all = ssd_buf[g] + jnp.dot(sp_ref[...], jnp.concatenate(free_all, axis=1),
                                      preferred_element_type=f32)
        for k in range(GROUP):
            e = g * GROUP + k
            wf = free_all[k]
            wd = node_major(ud, k)
            ss = ss_all[:, k * samples:(k + 1) * samples]
            tot = wf.astype(f32) + wd.astype(f32)
            lane = lax.broadcasted_iota(jnp.int32, tot.shape, 1)
            prev = jnp.where(lane == 0, 0.0, pltpu.roll(tot, 1, 1))
            nxt = jnp.where(lane == samples - 1, 0.0, pltpu.roll(tot, samples - 1, 1))
            accel = (nxt - 2.0 * tot) + prev
            f = sc_ref[e] * ss + mc_ref[e] * accel
            forces.append(
                jnp.concatenate([f[c * nodes:(c + 1) * nodes, :] for c in range(3)], axis=1))
        fg = jnp.concatenate(forces, axis=0)
        hi = fg.astype(bf16)
        lo = (fg - hi.astype(f32)).astype(bf16)
        hi_buf[rows, :] = hi
        lo_buf[rows, :] = lo
        both = jnp.dot(ohtf_buf[g], jnp.concatenate([hi, lo], axis=1),
                       preferred_element_type=f32)
        back[...] += both[:, :3 * samples] + both[:, 3 * samples:]
        return carry

    def dam_scatter(g, carry):
        rows = pl.ds(pl.multiple_of(g * width, width), width)
        both = jnp.dot(ohtd_buf[g], jnp.concatenate([hi_buf[rows, :], lo_buf[rows, :]], axis=1),
                       preferred_element_type=f32)
        dsum[...] += both[:, :3 * samples] + both[:, 3 * samples:]
        return carry

    hist_out[...] = hist_ref[...]
    dam_out[...] = dam_ref[...]
    for r in range(ROUNDS):
        base_f, base_b = 1 + 6 * r, 4 + 6 * r
        outgoing = jnp.dot(qt_ref[...], hist_out[...], preferred_element_type=f32).astype(bf16)
        stage_f[...] = outgoing.reshape(blocks)
        own_f = start_exchange(stage_f, lands_f[r], base_f)
        gather_all(ohd_buf, dam_out, ud_buf)
        lax.fori_loop(0, groups, dam_side, 0)
        finish_exchange(stage_f, lands_f[r], base_f, own_f)
        local_copy(lands_f[r], landv_f)
        recv[...] = landv_f[...].reshape(recv.shape)

        back[...] = jnp.zeros(back.shape, f32)
        gather_all(ohf_buf, recv, uf_buf)
        lax.fori_loop(0, groups, free_side, 0)
        stage_b[...] = back[...].reshape(blocks)
        own_b = start_exchange(stage_b, lands_b[r], base_b)
        dsum[...] = jnp.zeros(dsum.shape, f32)
        lax.fori_loop(0, groups, dam_scatter, 0)
        dam_out[...] = (dam_out[...].astype(f32) - dstep_ref[...] * dsum[...]).astype(bf16)
        finish_exchange(stage_b, lands_b[r], base_b, own_b)
        local_copy(lands_b[r], landv_b)
        ret[...] = landv_b[...].reshape(ret.shape)

        returned = ret[...]
        ret_hi = returned.astype(bf16)
        ret_lo = (returned - ret_hi.astype(f32)).astype(bf16)
        pulled = (jnp.dot(q_ref[...], ret_hi, preferred_element_type=f32)
                  + jnp.dot(q_ref[...], ret_lo, preferred_element_type=f32))
        hist_out[...] = (hist_out[...].astype(f32) - rstep_ref[...] * pulled).astype(bf16)
        if r == ROUNDS - 1:
            pulled_out[...] = pulled


def shards(history, routes, dam_field, conn_free, conn_dam, stiff_ref, stiff_coef,
           mass_coef, reg_step, dam_step):
    devices = lax.axis_size(("reg", "dam"))
    ndam = lax.axis_size("dam")
    row_count, row_width = history.shape
    capacity = 4 * row_count // devices
    slots = devices * capacity
    nodes = conn_free.shape[1]
    samples = row_width // 3
    smem = pl.BlockSpec(memory_space=pltpu.SMEM)
    vmem = pl.BlockSpec(memory_space=pltpu.VMEM)
    anywhere = pl.BlockSpec(memory_space=pl.ANY)
    elements = conn_free.shape[0]
    groups = conn_free.shape[0] // GROUP
    hbm_f = jax.ShapeDtypeStruct((devices, capacity, row_width), jnp.bfloat16)
    hbm_b = jax.ShapeDtypeStruct((devices, capacity, row_width), jnp.float32)
    outs = pl.pallas_call(
        functools.partial(coupling_kernel, devices, ndam),
        out_shape=(
            jax.ShapeDtypeStruct(history.shape, jnp.bfloat16),
            jax.ShapeDtypeStruct(history.shape, jnp.float32),
            jax.ShapeDtypeStruct(dam_field.shape, jnp.bfloat16),
            hbm_f, hbm_f, hbm_b, hbm_b,
        ),
        in_specs=[smem, smem] + [vmem] * 8,
        out_specs=(vmem, vmem, vmem) + (anywhere,) * 4,
        scratch_shapes=[
            pltpu.VMEM(hbm_f.shape, jnp.bfloat16),
            pltpu.VMEM(hbm_b.shape, jnp.float32),
            pltpu.VMEM(hbm_f.shape, jnp.bfloat16),
            pltpu.VMEM(hbm_b.shape, jnp.float32),
            pltpu.VMEM((slots, row_width), jnp.bfloat16),
            pltpu.VMEM((elements * nodes, row_width), jnp.bfloat16),
            pltpu.VMEM((groups, 3 * nodes, GROUP * samples), jnp.float32),
            pltpu.VMEM((elements * nodes, row_width), jnp.bfloat16),
            pltpu.VMEM((elements * nodes, row_width), jnp.bfloat16),
            pltpu.VMEM((slots, row_width), jnp.float32),
            pltpu.VMEM(dam_field.shape, jnp.float32),
            pltpu.VMEM((slots, row_width), jnp.float32),
            pltpu.VMEM((elements * nodes, slots), jnp.bfloat16),
            pltpu.VMEM((elements * nodes, dam_field.shape[0]), jnp.bfloat16),
            pltpu.VMEM((groups, slots, GROUP * nodes), jnp.bfloat16),
            pltpu.VMEM((groups, dam_field.shape[0], GROUP * nodes), jnp.bfloat16),
            pltpu.VMEM((elements * nodes, row_width), jnp.bfloat16),
            pltpu.VMEM(stiff_ref.shape, jnp.bfloat16),
            pltpu.VMEM((row_count, slots), jnp.bfloat16),
            pltpu.VMEM((slots, row_count), jnp.bfloat16),
            pltpu.VMEM((dam_field.shape[0], 1), jnp.float32),
            pltpu.VMEM((row_count, 1), jnp.float32),
            pltpu.SemaphoreType.DMA((1 + 6 * ROUNDS,)),
        ],
        compiler_params=pltpu.CompilerParams(
            collective_id=0, has_side_effects=True, vmem_limit_bytes=60 * 1024 * 1024),
    )(stiff_coef, mass_coef, history, dam_field, conn_free, conn_dam, stiff_ref,
      dam_step.reshape(1, -1), reg_step.reshape(1, -1), jnp.transpose(routes))
    return (outs[0], outs[1], outs[2])


def solution(mesh):
    in_specs = (
        P(("reg", "dam"), None),
        P(("reg", "dam"), None),
        P(("reg", "dam"), None),
        P(("reg", "dam"), None),
        P(("reg", "dam"), None),
        P(),
        P(("reg", "dam")),
        P(("reg", "dam")),
        P(("reg", "dam")),
        P(("reg", "dam")),
    )
    out_specs = (P(("reg", "dam"), None), P(("reg", "dam"), None), P(("reg", "dam"), None))
    return jax.shard_map(shards, mesh=mesh, in_specs=in_specs, out_specs=out_specs, check_vma=False)
```

```python
import functools

import jax
import jax.numpy as jnp
from jax import lax
from jax.experimental import pallas as pl
from jax.experimental.pallas import tpu as pltpu
from jax.sharding import PartitionSpec as P

ROUNDS = 2
GROUP = 32
GATHER_PARTS = 4


def coupling_kernel(n, ndam, sc_ref, mc_ref, hist_ref, dam_ref, cf_ref, cd_ref, stiff_ref,
                    dstep_row, rstep_row, routes_ref,
                    hist_out, pulled_out, dam_out,
                    land_f0, land_f1, land_b0, land_b1,
                    stage_f, stage_b, landv_f, landv_b,
                    recv, ud_buf, ssd_buf, hi_buf, lo_buf, back, dsum, ret,
                    ohf_buf, ohd_buf, ohtf_buf, ohtd_buf, uf_buf, sp_ref, q_ref, qt_ref, dstep_ref, rstep_ref,
                    sems):
    f32, bf16 = jnp.float32, jnp.bfloat16
    mesh_id = pl.DeviceIdType.MESH
    me = lax.axis_index("reg") * ndam + lax.axis_index("dam")
    slots = recv.shape[0]
    dcount = dam_out.shape[0]
    nodes = cf_ref.shape[1]
    width = GROUP * nodes
    groups = cf_ref.shape[0] // GROUP
    samples = recv.shape[1] // 3
    lands_f, lands_b = (land_f0, land_f1), (land_b0, land_b1)
    blocks = stage_f.shape

    barrier = pltpu.get_barrier_semaphore()

    def greet(step, carry):
        peer = lax.rem(me + step, n)
        pl.semaphore_signal(barrier, 1, device_id=(peer // ndam, peer % ndam),
                            device_id_type=mesh_id)
        return carry

    lax.fori_loop(1, n, greet, 0)

    def build_selectors(g, carry):
        for k in range(GROUP):
            lanes = slice(k * nodes, (k + 1) * nodes)
            cf = cf_ref[pl.ds(g * GROUP + k, 1), :]
            cd = cd_ref[pl.ds(g * GROUP + k, 1), :]
            ohtf_buf[g, :, lanes] = (
                lax.broadcasted_iota(jnp.int32, (slots, nodes), 0) == cf).astype(bf16)
            ohtd_buf[g, :, lanes] = (
                lax.broadcasted_iota(jnp.int32, (dcount, nodes), 0) == cd).astype(bf16)
        rows = pl.ds(pl.multiple_of(g * width, width), width)
        ohf_buf[rows, :] = jnp.transpose(ohtf_buf[g].astype(f32)).astype(bf16)
        ohd_buf[rows, :] = jnp.transpose(ohtd_buf[g].astype(f32)).astype(bf16)
        return carry

    lax.fori_loop(0, groups, build_selectors, 0)
    size = sp_ref.shape[0]
    across = lax.broadcasted_iota(jnp.int32, (size, size), 0)
    down = lax.broadcasted_iota(jnp.int32, (size, size), 1)
    pick_rows = (down == (across % nodes) * 3 + across // nodes).astype(bf16)
    pick_cols = (across == (down % nodes) * 3 + down // nodes).astype(bf16)
    permuted = jnp.dot(pick_rows, stiff_ref[...], preferred_element_type=f32).astype(bf16)
    sp_ref[...] = jnp.dot(permuted, pick_cols, preferred_element_type=f32).astype(bf16)
    regional = routes_ref.shape[1]
    capacity = slots // n
    first = routes_ref[0:1, :]
    second = routes_ref[1:2, :]
    numbers = lax.broadcasted_iota(jnp.int32, (n, regional), 0)
    hit_first = (first == numbers).astype(f32)
    hit_second = (second == numbers).astype(f32)
    earlier = (lax.broadcasted_iota(jnp.int32, (regional, regional), 0)
               < lax.broadcasted_iota(jnp.int32, (regional, regional), 1)).astype(bf16)
    counts = jnp.dot((hit_first + hit_second).astype(bf16), earlier, preferred_element_type=f32)
    slot_first = jnp.sum(counts * hit_first, axis=0, keepdims=True).astype(jnp.int32)
    slot_second = jnp.sum(counts * hit_second, axis=0, keepdims=True).astype(jnp.int32)
    place_first = first * capacity + slot_first
    place_second = second * capacity + slot_second
    positions = lax.broadcasted_iota(jnp.int32, (slots, regional), 0)
    pair = jnp.logical_or(positions == place_first, positions == place_second).astype(f32)
    qt_ref[...] = pair.astype(bf16)
    q_ref[...] = jnp.transpose(pair).astype(bf16)
    dstep_ref[...] = jnp.transpose(
        jnp.broadcast_to(dstep_row[...], (8, dstep_row.shape[1])))[:, 0:1]
    rstep_ref[...] = jnp.transpose(
        jnp.broadcast_to(rstep_row[...], (8, rstep_row.shape[1])))[:, 0:1]
    pl.semaphore_wait(barrier, n - 1)

    def local_copy(src, dst):
        cp = pltpu.make_async_copy(src, dst, sems.at[0])
        cp.start()
        cp.wait()

    def start_exchange(stage, land, base):
        own = pltpu.make_async_copy(stage.at[me], land.at[me], sems.at[base + 2])
        own.start()

        def send(step, carry):
            peer = lax.rem(me + step, n)
            pltpu.make_async_remote_copy(
                src_ref=stage.at[peer],
                dst_ref=land.at[me],
                send_sem=sems.at[base],
                recv_sem=sems.at[base + 1],
                device_id=(peer // ndam, peer % ndam),
                device_id_type=mesh_id,
            ).start()
            return carry

        lax.fori_loop(1, n, send, 0)
        return own

    def finish_exchange(stage, land, base, own):
        everything = pltpu.make_async_remote_copy(
            src_ref=stage.at[pl.ds(0, n - 1)],
            dst_ref=land.at[pl.ds(0, n - 1)],
            send_sem=sems.at[base],
            recv_sem=sems.at[base + 1],
            device_id=(me // ndam, me % ndam),
            device_id_type=mesh_id,
        )
        everything.wait_send()
        everything.wait_recv()
        own.wait()

    def node_major(u, k):
        lo_row, hi_row = k * nodes, (k + 1) * nodes
        return jnp.concatenate(
            [u[lo_row:hi_row, c * samples:(c + 1) * samples] for c in range(3)], axis=0)

    def gather_all(select, table, out):
        for part in range(GATHER_PARTS):
            rows = slice(part * out.shape[0] // GATHER_PARTS, (part + 1) * out.shape[0] // GATHER_PARTS)
            out[rows, :] = jnp.dot(select[rows, :], table[...],
                                   preferred_element_type=f32).astype(bf16)

    def dam_side(g, carry):
        rows = pl.ds(pl.multiple_of(g * width, width), width)
        ud = ud_buf[rows, :]
        side = jnp.concatenate([node_major(ud, k) for k in range(GROUP)], axis=1)
        ssd_buf[g] = jnp.dot(sp_ref[...], side, preferred_element_type=f32)
        return carry

    def free_side(g, carry):
        rows = pl.ds(pl.multiple_of(g * width, width), width)
        uf = uf_buf[rows, :]
        ud = ud_buf[rows, :]
        forces = []
        free_all = [node_major(uf, k) for k in range(GROUP)]
        ss_all = ssd_buf[g] + jnp.dot(sp_ref[...], jnp.concatenate(free_all, axis=1),
                                      preferred_element_type=f32)
        for k in range(GROUP):
            e = g * GROUP + k
            wf = free_all[k]
            wd = node_major(ud, k)
            ss = ss_all[:, k * samples:(k + 1) * samples]
            tot = wf.astype(f32) + wd.astype(f32)
            lane = lax.broadcasted_iota(jnp.int32, tot.shape, 1)
            prev = jnp.where(lane == 0, 0.0, pltpu.roll(tot, 1, 1))
            nxt = jnp.where(lane == samples - 1, 0.0, pltpu.roll(tot, samples - 1, 1))
            accel = (nxt - 2.0 * tot) + prev
            f = sc_ref[e] * ss + mc_ref[e] * accel
            forces.append(
                jnp.concatenate([f[c * nodes:(c + 1) * nodes, :] for c in range(3)], axis=1))
        fg = jnp.concatenate(forces, axis=0)
        hi = fg.astype(bf16)
        lo = (fg - hi.astype(f32)).astype(bf16)
        hi_buf[rows, :] = hi
        lo_buf[rows, :] = lo
        both = jnp.dot(ohtf_buf[g], jnp.concatenate([hi, lo], axis=1),
                       preferred_element_type=f32)
        back[...] += both[:, :3 * samples] + both[:, 3 * samples:]
        return carry

    def dam_scatter(g, carry):
        rows = pl.ds(pl.multiple_of(g * width, width), width)
        both = jnp.dot(ohtd_buf[g], jnp.concatenate([hi_buf[rows, :], lo_buf[rows, :]], axis=1),
                       preferred_element_type=f32)
        dsum[...] += both[:, :3 * samples] + both[:, 3 * samples:]
        return carry

    hist_out[...] = hist_ref[...]
    dam_out[...] = dam_ref[...]
    for r in range(ROUNDS):
        base_f, base_b = 1 + 6 * r, 4 + 6 * r
        outgoing = jnp.dot(qt_ref[...], hist_out[...], preferred_element_type=f32).astype(bf16)
        stage_f[...] = outgoing.reshape(blocks)
        own_f = start_exchange(stage_f, lands_f[r], base_f)
        gather_all(ohd_buf, dam_out, ud_buf)
        lax.fori_loop(0, groups, dam_side, 0)
        finish_exchange(stage_f, lands_f[r], base_f, own_f)
        local_copy(lands_f[r], landv_f)
        recv[...] = landv_f[...].reshape(recv.shape)

        back[...] = jnp.zeros(back.shape, f32)
        gather_all(ohf_buf, recv, uf_buf)
        lax.fori_loop(0, groups, free_side, 0)
        stage_b[...] = back[...].reshape(blocks)
        own_b = start_exchange(stage_b, lands_b[r], base_b)
        dsum[...] = jnp.zeros(dsum.shape, f32)
        lax.fori_loop(0, groups, dam_scatter, 0)
        dam_out[...] = (dam_out[...].astype(f32) - dstep_ref[...] * dsum[...]).astype(bf16)
        finish_exchange(stage_b, lands_b[r], base_b, own_b)
        local_copy(lands_b[r], landv_b)
        ret[...] = landv_b[...].reshape(ret.shape)

        returned = ret[...]
        ret_hi = returned.astype(bf16)
        ret_lo = (returned - ret_hi.astype(f32)).astype(bf16)
        pulled = (jnp.dot(q_ref[...], ret_hi, preferred_element_type=f32)
                  + jnp.dot(q_ref[...], ret_lo, preferred_element_type=f32))
        hist_out[...] = (hist_out[...].astype(f32) - rstep_ref[...] * pulled).astype(bf16)
        if r == ROUNDS - 1:
            pulled_out[...] = pulled


def shards(history, routes, dam_field, conn_free, conn_dam, stiff_ref, stiff_coef,
           mass_coef, reg_step, dam_step):
    devices = lax.axis_size(("reg", "dam"))
    ndam = lax.axis_size("dam")
    row_count, row_width = history.shape
    capacity = 4 * row_count // devices
    slots = devices * capacity
    nodes = conn_free.shape[1]
    samples = row_width // 3
    smem = pl.BlockSpec(memory_space=pltpu.SMEM)
    vmem = pl.BlockSpec(memory_space=pltpu.VMEM)
    anywhere = pl.BlockSpec(memory_space=pl.ANY)
    elements = conn_free.shape[0]
    groups = conn_free.shape[0] // GROUP
    hbm_f = jax.ShapeDtypeStruct((devices, capacity, row_width), jnp.bfloat16)
    hbm_b = jax.ShapeDtypeStruct((devices, capacity, row_width), jnp.float32)
    outs = pl.pallas_call(
        functools.partial(coupling_kernel, devices, ndam),
        out_shape=(
            jax.ShapeDtypeStruct(history.shape, jnp.bfloat16),
            jax.ShapeDtypeStruct(history.shape, jnp.float32),
            jax.ShapeDtypeStruct(dam_field.shape, jnp.bfloat16),
            hbm_f, hbm_f, hbm_b, hbm_b,
        ),
        in_specs=[smem, smem] + [vmem] * 8,
        out_specs=(vmem, vmem, vmem) + (anywhere,) * 4,
        scratch_shapes=[
            pltpu.VMEM(hbm_f.shape, jnp.bfloat16),
            pltpu.VMEM(hbm_b.shape, jnp.float32),
            pltpu.VMEM(hbm_f.shape, jnp.bfloat16),
            pltpu.VMEM(hbm_b.shape, jnp.float32),
            pltpu.VMEM((slots, row_width), jnp.bfloat16),
            pltpu.VMEM((elements * nodes, row_width), jnp.bfloat16),
            pltpu.VMEM((groups, 3 * nodes, GROUP * samples), jnp.float32),
            pltpu.VMEM((elements * nodes, row_width), jnp.bfloat16),
            pltpu.VMEM((elements * nodes, row_width), jnp.bfloat16),
            pltpu.VMEM((slots, row_width), jnp.float32),
            pltpu.VMEM(dam_field.shape, jnp.float32),
            pltpu.VMEM((slots, row_width), jnp.float32),
            pltpu.VMEM((elements * nodes, slots), jnp.bfloat16),
            pltpu.VMEM((elements * nodes, dam_field.shape[0]), jnp.bfloat16),
            pltpu.VMEM((groups, slots, GROUP * nodes), jnp.bfloat16),
            pltpu.VMEM((groups, dam_field.shape[0], GROUP * nodes), jnp.bfloat16),
            pltpu.VMEM((elements * nodes, row_width), jnp.bfloat16),
            pltpu.VMEM(stiff_ref.shape, jnp.bfloat16),
            pltpu.VMEM((row_count, slots), jnp.bfloat16),
            pltpu.VMEM((slots, row_count), jnp.bfloat16),
            pltpu.VMEM((dam_field.shape[0], 1), jnp.float32),
            pltpu.VMEM((row_count, 1), jnp.float32),
            pltpu.SemaphoreType.DMA((1 + 6 * ROUNDS,)),
        ],
        compiler_params=pltpu.CompilerParams(
            collective_id=0, has_side_effects=True, vmem_limit_bytes=60 * 1024 * 1024),
    )(stiff_coef, mass_coef, history, dam_field, conn_free, conn_dam, stiff_ref,
      dam_step.reshape(1, -1), reg_step.reshape(1, -1), jnp.transpose(routes))
    return (outs[0], outs[1], outs[2])


def solution(mesh):
    in_specs = (
        P(("reg", "dam"), None),
        P(("reg", "dam"), None),
        P(("reg", "dam"), None),
        P(("reg", "dam"), None),
        P(("reg", "dam"), None),
        P(),
        P(("reg", "dam")),
        P(("reg", "dam")),
        P(("reg", "dam")),
        P(("reg", "dam")),
    )
    out_specs = (P(("reg", "dam"), None), P(("reg", "dam"), None), P(("reg", "dam"), None))
    return jax.shard_map(shards, mesh=mesh, in_specs=in_specs, out_specs=out_specs, check_vma=False)
```
